256 devices in a mesh: gx: 32 (over z_hi, x, core), gy: 8 (over y, z_lo).
Axes of the slice: x: 4, y: 4, z: 8 (z_hi: 4, z_lo: 2; z = z_hi * 2 + z_lo), core: 2. Of those that a mesh axis runs over, the one named last changes fastest.
Arguments:
- populations: float32 [19, 16, 512, 1024], P(None, None, 'gx', 'gy'), as said below
- solid_mask: int32 [16, 512, 1024], P(None, 'gx', 'gy'), may hold values 0 or 1
- bead_states: float32 [32, 8, 8, 9, 1280], P('gx', 'gy'), as said below
- bead_bricks: int32 [32, 8, 8, 20], P('gx', 'gy'), may hold values from 0 to 63, as said below
- leave_dir: int32 [32, 8, 8], P('gx', 'gy'), may hold values from 0 to 4, as said below
- stiffness: bfloat16 [1280, 1280], replicated, may hold values from -0.15625 to 0.15625
Outputs:
- populations_out: float32 [19, 16, 512, 1024], P(None, None, 'gx', 'gy')
- vertex_out: float32 [32, 8, 16, 9, 1280], P('gx', 'gy')
The draws below stay inside these ranges and needn't reach their ends.
Inputs may be any that keep to these rules, and one draw needn't show every extreme that they name: `populations`: every entry is positive. `bead_states`: in the second dimension from the end, entries 0 to 2 are a vertex's x, y, z cell coordinates inside its block's brick, from 1 to 6; entries 3 to 5 its displacement from the reference shape; entries 6 to 8 its velocity. Every slot holds a bead. `bead_bricks`: a brick index counted in the tile that holds the bead after migration. `leave_dir`: 0 keeps the bead on its tile; 1 and 2 move it to the next tile along +x and -x, 3 and 4 along +y and -y. On every tile at most 2 beads have any one code from 1 to 4, and exactly 2 have one of them.
All inputs are finite; a program needn't handle non-finite values. No bound on the sum of `solid_mask` on one device may be relied on, other than what follows from the above.
Results may differ from the reference program's by a relative error of at most 0.00036.
Values sent between devices are 32-bit elements; how exact they have to be, the bound alone decides.
No kernel may reach another device: no remote copies, remote signals or barrier semaphores. Data moves between devices by JAX's collectives and lax.ppermute only.
A program may use at most 128 MiB of HBM per device.

```python
from functools import partial
import jax
import jax.numpy as jnp
import numpy as np
from jax import lax

VERTICES = 1280
BLOCKS = 20
NZ = 16
CX = 16
CY = 128
SLOTS = 8
MIG = 2
ALL_SLOTS = 16
BRICKS = 64
NX = 512
NY = 1024
N_GX = 32
N_GY = 8


WEIGHTS = np.array([1.0 / 3.0] + [1.0 / 18.0] * 6 + [1.0 / 36.0] * 12)


def draw_populations(key, part):
    weights = jnp.asarray(WEIGHTS, jnp.float32).reshape(19, 1, 1, 1)
    shape = (19, NZ, NX, NY)
    noise = jnp.clip(jax.random.normal(key, shape, jnp.float32), -3.0, 3.0)
    return weights * (1.0 + 0.3 * noise)


def draw_bead_states(key, part):
    shape = (N_GX, N_GY, SLOTS, 3, VERTICES)
    first_key, second_key, third_key = jax.random.split(key, 3)
    offsets = jax.random.uniform(first_key, shape, jnp.float32, 1.0, 6.0)
    displacement = 0.3 * jnp.clip(jax.random.normal(second_key, shape, jnp.float32), -4.0, 4.0)
    velocity = 0.05 * jnp.clip(jax.random.normal(third_key, shape, jnp.float32), -4.0, 4.0)
    return jnp.concatenate([offsets, displacement, velocity], axis=3)


def draw_bead_bricks(key, part):
    drawn = jax.random.randint(key, (N_GX, N_GY, SLOTS, BLOCKS), 0, BRICKS, dtype=jnp.int32)
    drawn = drawn.at[0, 0, 0, 0].set(BRICKS - 1)
    drawn = drawn.at[0, 0, 0, BLOCKS - 1].set(0)
    return drawn.astype(jnp.int32)


def draw_leave_dir(key, part):
    tile_count = N_GX * N_GY
    key_list = jax.random.split(key, tile_count)

    def one_tile(tile_key, tile_number):
        perm_key, count_key = jax.random.split(tile_key)
        slot_counts = jax.random.randint(count_key, (4,), 0, MIG, dtype=jnp.int32)
        full_code = tile_number % 4
        slot_counts = jnp.where(jnp.arange(4) == full_code, MIG, slot_counts)
        limits = jnp.cumsum(slot_counts)
        positions = jnp.arange(SLOTS)
        direction_codes = 1 + jnp.sum((positions[:, None] >= limits[None, :]).astype(jnp.int32), axis=1)
        direction_codes = jnp.where(direction_codes == 5, 0, direction_codes).astype(jnp.int32)
        ordering = jax.random.permutation(perm_key, SLOTS)
        return jnp.zeros((SLOTS,), jnp.int32).at[ordering].set(direction_codes)
    result = jax.vmap(one_tile)(key_list, jnp.arange(tile_count, dtype=jnp.int32))
    return result.reshape(N_GX, N_GY, SLOTS).astype(jnp.int32)


def place_ends(values, own_key, smallest, largest):
    place = [jax.random.randint(jax.random.fold_in(own_key, axis), (), 0, length) for axis, length in enumerate(values.shape)]
    longest = values.shape.index(max(values.shape))
    neighbour = place[:longest] + [(place[longest] + 1) % values.shape[longest]] + place[longest + 1:]
    return values.at[tuple(place)].set(smallest).at[tuple(neighbour)].set(largest)


def gaussian(rng, shape, scale, most, kind=jnp.bfloat16):
    entries = scale * jax.random.normal(rng, shape, jnp.float32)
    return jnp.clip(entries, min=-most, max=most).astype(kind)


def setup_inputs(seed: int = 0) -> dict:
    keys = jax.random.split(jax.random.key(seed), 7)
    populations = draw_populations(jax.random.fold_in(keys[6], 71), 0)
    solid_mask = place_ends((jax.random.randint(keys[1], (NZ, NX, NY), 0, 4) < 1).astype(jnp.int32), jax.random.fold_in(keys[1], 1), 0, 1)
    bead_states = draw_bead_states(jax.random.fold_in(keys[6], 71), 0)
    bead_bricks = draw_bead_bricks(jax.random.fold_in(keys[6], 71), 0)
    leave_dir = draw_leave_dir(jax.random.fold_in(keys[6], 71), 0)
    stiffness = gaussian(keys[5], (VERTICES, VERTICES), VERTICES ** -0.5, 0.15625)
    return {"populations": populations, "solid_mask": solid_mask, "bead_states": bead_states, "bead_bricks": bead_bricks, "leave_dir": leave_dir, "stiffness": stiffness}


LATTICE = np.array([[0, 0, 0], [1, 0, 0], [-1, 0, 0], [0, 1, 0], [0, -1, 0], [0, 0, 1], [0, 0, -1], [1, 1, 0], [-1, -1, 0], [1, -1, 0], [-1, 1, 0], [1, 0, 1], [-1, 0, -1], [1, 0, -1], [-1, 0, 1], [0, 1, 1], [0, -1, -1], [0, 1, -1], [0, -1, 1]])
OPPOSITE = [0, 2, 1, 4, 3, 6, 5, 8, 7, 10, 9, 12, 11, 14, 13, 16, 15, 18, 17]
WEIGHTS = np.array([1.0 / 3.0] + [1.0 / 18.0] * 6 + [1.0 / 36.0] * 12)
RELAX_TIME = 0.8
HIGHEST = lax.Precision.HIGHEST


def kernel_weight(distance):
    inside = jnp.abs(distance) < 2.0
    return jnp.where(inside, 0.25 * (1.0 + jnp.cos(0.5 * jnp.pi * distance)), 0.0 * distance)


def block_weights(block_offsets):
    cell_steps = jnp.arange(8).astype(block_offsets.dtype)
    factors = kernel_weight(block_offsets[:, :, :, None] - cell_steps)
    along_x = factors[:, 0]
    along_y = factors[:, 1]
    along_z = factors[:, 2]
    weight_table = along_z[:, :, :, None, None] * along_x[:, :, None, :, None] * along_y[:, :, None, None, :]
    return weight_table.reshape(block_offsets.shape[0], 64, 512)


def moments(read):
    lattice = jnp.asarray(LATTICE, read.dtype)
    density = jnp.sum(read, axis=0)
    momentum = jnp.tensordot(lattice.T, read, axes=1, precision=HIGHEST)
    return density, momentum


def collide(read, momentum, density, force, solid_mask):
    lattice = jnp.asarray(LATTICE, read.dtype)
    weights = jnp.asarray(WEIGHTS, read.dtype).reshape(19, 1, 1, 1)
    velocity = (momentum + 0.5 * force) / density
    projected = jnp.tensordot(lattice, velocity, axes=1, precision=HIGHEST)
    force_along = jnp.tensordot(lattice, force, axes=1, precision=HIGHEST)
    speed_square = jnp.sum(velocity * velocity, axis=0)
    force_dot = jnp.sum(velocity * force, axis=0)
    equilibrium = weights * density * (1.0 + 3.0 * projected + 4.5 * projected * projected - 1.5 * speed_square)
    source = weights * (3.0 * force_along - 3.0 * force_dot + 9.0 * projected * force_along)
    relaxed = read - (read - equilibrium) / RELAX_TIME + (1.0 - 0.5 / RELAX_TIME) * source
    bounced = jnp.stack([read[lattice_index] for lattice_index in OPPOSITE])
    return jnp.where(solid_mask[None] == 1, bounced, relaxed)


def to_bricks(field):
    depth, width, height = field.shape[1], field.shape[2], field.shape[3]
    blocked = field.reshape(3, depth // 8, 8, width // 8, 8, height // 8, 8)
    blocked = blocked.transpose(1, 3, 5, 0, 2, 4, 6)
    return blocked.reshape(-1, 3, 512)


def from_bricks(blocked, depth, width, height):
    shaped = blocked.reshape(depth // 8, width // 8, height // 8, 3, 8, 8, 8)
    shaped = shaped.transpose(3, 0, 4, 1, 5, 2, 6)
    return shaped.reshape(3, depth, width, height)


def outbox(states, bricks, leaving, code):
    chosen = (leaving == code).astype(jnp.int32)
    ranking = jnp.cumsum(chosen) - 1
    targets = jnp.arange(MIG)
    picker = ((chosen[None, :] == 1) & (ranking[None, :] == targets[:, None])).astype(states.dtype)
    moved = jnp.einsum('ms,scv->mcv', picker, states, precision=HIGHEST)
    moved_bricks = jnp.einsum('ms,sb->mb', picker, bricks.astype(states.dtype), precision=HIGHEST)
    valid = jnp.sum(picker, axis=1)
    return moved, moved_bricks, valid


def couple_tile(velocity_bricks, states, bricks, active, stiffness):
    slot_count = states.shape[0]
    vertices = states.shape[2]
    per_slot = vertices // 64
    displacement = states[:, 3:6, :].astype(jnp.bfloat16)
    product = jnp.dot(displacement.reshape(slot_count * 3, vertices).astype(jnp.float32), stiffness.astype(jnp.float32), precision=HIGHEST)
    node_force = -product.reshape(slot_count, 3, vertices) * active[:, None, None]
    force_sample = node_force.astype(jnp.bfloat16).astype(states.dtype)
    velocity_sample = velocity_bricks.astype(jnp.bfloat16).astype(states.dtype)

    def blockify(values):
        shaped = values.reshape(slot_count, 3, per_slot, 64).transpose(0, 2, 1, 3)
        return shaped.reshape(slot_count * per_slot, 3, 64)

    groups = 8
    block_total = slot_count * per_slot
    group_size = block_total // groups
    positions = blockify(states[:, 0:3, :]).reshape(groups, group_size, 3, 64)
    forces = blockify(force_sample).reshape(groups, group_size, 3, 64)
    brick_list = bricks.reshape(groups, group_size).astype(jnp.int32)

    def couple_group(brick_force, pieces):
        block_offsets, block_force, where_brick = pieces
        weight_table = block_weights(block_offsets).astype(jnp.bfloat16).astype(block_offsets.dtype)
        nearby = velocity_sample[where_brick]
        sampled = jnp.einsum('bcq,bvq->bcv', nearby, weight_table, precision=HIGHEST)
        spread = jnp.einsum('bcv,bvq->bcq', block_force, weight_table, precision=HIGHEST)
        brick_force = brick_force.at[where_brick].add(spread)
        return brick_force, sampled

    start_force = jnp.zeros(velocity_bricks.shape, node_force.dtype)
    brick_force, sampled = lax.scan(couple_group, start_force, (positions, forces, brick_list))
    vertex_velocity = sampled.reshape(slot_count, per_slot, 3, 64).transpose(0, 2, 1, 3).reshape(slot_count, 3, vertices)
    half_step = 0.5 * (states[:, 6:9, :] + vertex_velocity)
    result = jnp.concatenate([states[:, 0:3, :] + half_step, states[:, 3:6, :] + half_step, vertex_velocity], axis=1)
    return brick_force, result * active[:, None, None]


def migrate(bead_states, bead_bricks, leave_dir):
    boxes = []
    for code in range(1, 5):
        boxes.append(jax.vmap(jax.vmap(partial(outbox, code=code)))(bead_states, bead_bricks, leave_dir))
    lower_x = jax.tree.map(partial(jnp.roll, shift=1, axis=0), boxes[0])
    upper_x = jax.tree.map(partial(jnp.roll, shift=-1, axis=0), boxes[1])
    lower_y = jax.tree.map(partial(jnp.roll, shift=1, axis=1), boxes[2])
    upper_y = jax.tree.map(partial(jnp.roll, shift=-1, axis=1), boxes[3])
    keeping = (leave_dir == 0).astype(bead_states.dtype)
    kept_states = bead_states * keeping[..., None, None]
    kept_bricks = bead_bricks.astype(bead_states.dtype) * keeping[..., None]
    received = [lower_x, upper_x, lower_y, upper_y]
    states = jnp.concatenate([kept_states] + [entry[0] for entry in received], axis=2)
    bricks = jnp.concatenate([kept_bricks] + [entry[1] for entry in received], axis=2)
    active = jnp.concatenate([keeping] + [entry[2] for entry in received], axis=2)
    return states, bricks.astype(jnp.int32), active


def reference(populations, solid_mask, bead_states, bead_bricks, leave_dir, stiffness):
    pulled = []
    for lattice_index in range(19):
        shift_x = int(LATTICE[lattice_index, 0])
        shift_y = int(LATTICE[lattice_index, 1])
        shift_z = int(LATTICE[lattice_index, 2])
        pulled.append(jnp.roll(populations[lattice_index], (shift_z, shift_x, shift_y), axis=(0, 1, 2)))
    read = jnp.stack(pulled)
    density, momentum = moments(read)
    fluid_velocity = momentum / density
    states, bricks, active = migrate(bead_states, bead_bricks, leave_dir)
    tile_count = N_GX * N_GY
    tile_velocity = fluid_velocity.reshape(3, NZ, N_GX, CX, N_GY, CY).transpose(2, 4, 0, 1, 3, 5).reshape(tile_count, 3, NZ, CX, CY)

    def per_tile(pieces):
        tile_field, tile_states, tile_bricks, tile_active = pieces
        return couple_tile(to_bricks(tile_field), tile_states, tile_bricks, tile_active, stiffness)

    brick_force, vertex_out = lax.map(per_tile, (tile_velocity, states.reshape(tile_count, ALL_SLOTS, 9, VERTICES), bricks.reshape(tile_count, ALL_SLOTS, BLOCKS), active.reshape(tile_count, ALL_SLOTS)))
    tile_force = jax.vmap(partial(from_bricks, depth=NZ, width=CX, height=CY))(brick_force)
    body_force = tile_force.reshape(N_GX, N_GY, 3, NZ, CX, CY).transpose(2, 3, 0, 4, 1, 5).reshape(3, NZ, NX, NY)
    populations_out = collide(read, momentum, density, body_force, solid_mask)
    return populations_out, vertex_out.reshape(N_GX, N_GY, ALL_SLOTS, 9, VERTICES)
```

```python
import functools

import jax
import jax.numpy as jnp
import numpy as np
from jax import lax
from jax.experimental import pallas as pl
from jax.experimental.pallas import tpu as pltpu
from jax.sharding import PartitionSpec as P

LATTICE = [
    (0, 0, 0),
    (1, 0, 0),
    (-1, 0, 0),
    (0, 1, 0),
    (0, -1, 0),
    (0, 0, 1),
    (0, 0, -1),
    (1, 1, 0),
    (-1, -1, 0),
    (1, -1, 0),
    (-1, 1, 0),
    (1, 0, 1),
    (-1, 0, -1),
    (1, 0, -1),
    (-1, 0, 1),
    (0, 1, 1),
    (0, -1, -1),
    (0, 1, -1),
    (0, -1, 1),
]
WEIGHTS = [1.0 / 3.0] + [1.0 / 18.0] * 6 + [1.0 / 36.0] * 12
X_UP = [1, 7, 9, 11, 13]
X_DOWN = [2, 8, 10, 12, 14]
Y_UP = [3, 7, 10, 15, 17]
Y_DOWN = [4, 8, 9, 16, 18]
CORNERS = [(7, 1, 1), (8, -1, -1), (9, 1, -1), (10, -1, 1)]

NZ, CX, CY = 16, 16, 128
SLOTS, SIDES, MIG, ALL = 8, 4, 2, 16
VERT, BLOCKS, CHUNK = 1280, 20, 256
F32, BF16 = jnp.float32, jnp.bfloat16


def lanes(shape):
    return lax.broadcasted_iota(jnp.int32, shape, len(shape) - 1)


def rows(shape):
    return lax.broadcasted_iota(jnp.int32, shape, len(shape) - 2)


def pack_kernel(leave, bricks, pops, states, *outs):
    faces, corners = outs[:4], outs[4:]
    lane = lanes((CX, CY))
    for side in range(4):
        out = faces[side]
        first, second, count = jnp.int32(0), jnp.int32(0), jnp.int32(0)
        for slot in range(SLOTS):
            hit = leave[0, 0, slot] == side + 1
            first = jnp.where(hit & (count == 0), slot, first)
            second = jnp.where(hit & (count == 1), slot, second)
            count = count + hit.astype(jnp.int32)
        for place, slot in enumerate((first, second)):
            out[8 * place : 8 * place + 8, :] = states[0, 0, slot, 0:8, :]
            out[16 + place : 17 + place, :] = states[0, 0, slot, 8:9, :]
            valid = (count > place).astype(F32)
            out[18 + place : 19 + place, 0:128] = jnp.full((1, 128), 1.0, F32) * valid
            out[18 + place : 19 + place, 0:BLOCKS] = bricks[0, 0, pl.ds(slot, 1), :].astype(F32)
    for side, (group, x) in enumerate(((X_UP, CX - 1), (X_DOWN, 0))):
        for i, q in enumerate(group):
            face = pops[q, pl.ds(x, NZ, stride=CX), :]
            for half in range(2):
                at = (half * 5 + i) * CY
                faces[side][24:32, at : at + CY] = face[8 * half : 8 * half + 8]
    columns = []
    for side, (group, y) in enumerate(((Y_UP, CY - 1), (Y_DOWN, 0))):
        column = jnp.zeros((CX, CY), F32)
        for i, q in enumerate(group):
            for z in range(NZ):
                plane = pops[q, z * CX : (z + 1) * CX, :]
                place = i * NZ + z
                column = jnp.where(lane == place, pltpu.roll(plane, (place - y) % CY, 1), column)
        faces[2 + side][24:32, 0:CY] = column[0:8]
        faces[2 + side][24:32, CY : 2 * CY] = column[8:16]
        columns.append(column)
    for out, (_, dx, dy) in zip(corners, CORNERS):
        column = columns[0 if dy > 0 else 1]
        out[...] = column[8:16] if dx > 0 else column[0:8]


def pack(leave, bricks, pops, states):
    vmem = pl.BlockSpec(memory_space=pltpu.VMEM)
    return pl.pallas_call(
        pack_kernel,
        out_shape=[jax.ShapeDtypeStruct((32, VERT), F32)] * 4
        + [jax.ShapeDtypeStruct((8, 128), F32)] * 4,
        in_specs=[pl.BlockSpec(memory_space=pltpu.SMEM), vmem, vmem, vmem],
        out_specs=[vmem] * 8,
        compiler_params=pltpu.CompilerParams(vmem_limit_bytes=32 << 20),
        name="pack_messages",
    )(leave, bricks, pops, states)


def phi(distance):
    t = distance * distance
    value = jnp.full(t.shape, COSINE[-1], F32)
    for coefficient in COSINE[-2::-1]:
        value = value * t + coefficient
    return jnp.where(jnp.abs(distance) < 2.0, 0.5 * (value * value), 0.0)


def cosine_terms():
    terms, term = [], 1.0
    for n in range(8):
        terms.append(float(term))
        term = -term * (np.pi / 4) ** 2 / ((2 * n + 1) * (2 * n + 2))
    return terms


COSINE = cosine_terms()


def step_kernel(
    leave, bricks, pops, solid, states,
    x_low, x_high, y_low, y_high, c_pp, c_mm, c_pm, c_mp,
    stiffness,
    pops_out, vertex_out,
    read, flow, halo_x, halo_y, turn, cells, force, moved, last, push, weights,
    meta, order, meta_sem, out_sem,
):
    faces = (x_low, x_high, y_low, y_high)
    copies = [
        pltpu.make_async_copy(faces[side].at[16:24, 0:128], meta.at[side], meta_sem.at[side])
        for side in range(4)
    ]
    for copy in copies:
        copy.start()

    for side in range(2):
        for i in range(5):
            for half in range(2):
                at = (half * 5 + i) * CY
                halo_x[side * 5 + i, 8 * half : 8 * half + 8, :] = faces[side][24:32, at : at + CY]
    row16 = rows((CX, CY))
    lane16 = lanes((CX, CY))
    corner = {7: (c_pp, 7), 8: (c_mm, 0), 9: (c_pm, 7), 10: (c_mp, 0)}
    for side, group in enumerate((Y_UP, Y_DOWN)):
        column = jnp.concatenate(
            [faces[2 + side][24:32, 0:CY], faces[2 + side][24:32, CY : 2 * CY]], axis=0
        )
        for i, q in enumerate(group):
            cx = LATTICE[q][0]
            if cx == 0:
                halo_y[side * 5 + i] = column
            else:
                source, row = corner[q]
                edge = jnp.broadcast_to(source[row : row + 1, :], (CX, CY))
                moved_column = pltpu.roll(column, cx % CX, 0)
                halo_y[side * 5 + i] = jnp.where(
                    row16 == (0 if cx > 0 else CX - 1), edge, moved_column
                )

    def pull(z, carry):
        density = None
        momentum = [None, None, None]
        at = pl.ds(pl.multiple_of(z * CX, CX), CX)
        for q in range(19):
            cx, cy, cz = LATTICE[q]
            source = (z - cz) & (NZ - 1)
            value = pops[q, pl.ds(pl.multiple_of(source * CX, CX), CX), :]
            if cx != 0:
                side, group = (0, X_UP) if cx > 0 else (1, X_DOWN)
                edge = halo_x[side * 5 + group.index(q), pl.ds(source, 1), :]
                value = jnp.where(
                    row16 == (0 if cx > 0 else CX - 1),
                    jnp.broadcast_to(edge, (CX, CY)),
                    pltpu.roll(value, cx % CX, 0),
                )
            if cy != 0:
                side, group = (0, Y_UP) if cy > 0 else (1, Y_DOWN)
                i = group.index(q)
                y = 0 if cy > 0 else CY - 1
                column = pltpu.roll(
                    halo_y[side * 5 + i], (y + 2 * CY - i * NZ - source) & (CY - 1), 1
                )
                value = jnp.where(lane16 == y, column, pltpu.roll(value, cy % CY, 1))
            read[q, at, :] = value
            density = value if density is None else density + value
            for k, c in enumerate((cx, cy, cz)):
                if c != 0:
                    signed = value if c > 0 else -value
                    momentum[k] = signed if momentum[k] is None else momentum[k] + signed
        inverse = 1.0 / density
        flow[0, at, :] = density
        for k in range(3):
            flow[1 + k, at, :] = momentum[k]
            flow[4 + k, at, :] = momentum[k] * inverse
        return carry

    lax.fori_loop(0, NZ, pull, 0)

    left = lanes((16, 128)) < 64
    for k in range(3):
        for bz in range(2):
            tiles = [
                flow[4 + k, (8 * bz + iz) * CX + 8 * bx : (8 * bz + iz) * CX + 8 * bx + 8, :]
                for bx in range(2)
                for iz in range(8)
            ]
            turn[...] = jnp.concatenate(tiles, axis=0).T
            for j in range(4):
                even = turn[pl.ds(2 * j, 16, stride=8), :]
                odd = turn[pl.ds(2 * j + 1, 16, stride=8), :]
                pairs = (
                    jnp.where(left, even, pltpu.roll(odd, 64, 1)),
                    jnp.where(left, pltpu.roll(even, 64, 1), odd),
                )
                for bx in range(2):
                    base = (bz * 2 + bx) * 16 * 8
                    cells[j, pl.ds(base + k, 16, stride=8), :] = pairs[bx]
                    cells[j, pl.ds(base + 3 + k, 16, stride=8), :] = pairs[bx]
                    if k < 2:
                        cells[j, pl.ds(base + 6 + k, 16, stride=8), :] = pairs[bx]

    for slot in range(SLOTS):
        moved[slot] = states[0, 0, slot, 0:8, :]
        last[slot : slot + 1, :] = states[0, 0, slot, 8:9, :]
    for side in range(4):
        for place in range(MIG):
            slot = SLOTS + side * MIG + place
            moved[slot] = faces[side][8 * place : 8 * place + 8, :]
            last[slot : slot + 1, :] = faces[side][16 + place : 17 + place, :]

    shape = moved[...].reshape(ALL * 8, VERT).astype(BF16)
    for n in range(5):
        at = slice(n * 256, (n + 1) * 256)
        push[:, at] = -jnp.dot(shape, stiffness[:, at], preferred_element_type=F32)

    force[...] = jnp.zeros(force.shape, F32)
    vertex_out[...] = jnp.zeros(vertex_out.shape, F32)

    for copy in copies:
        copy.wait()
    count = jnp.int32(0)
    for slot in range(SLOTS):
        order[count] = slot
        count = count + (leave[0, 0, slot] == 0).astype(jnp.int32)
    for side in range(4):
        for place in range(MIG):
            order[count] = SLOTS + side * MIG + place
            count = count + (meta[side, 2 + place, 64] > 0.5).astype(jnp.int32)

    row8 = rows((8, CHUNK))
    step8 = row8.astype(F32)
    lane8 = lanes((8, CHUNK))
    third = row8 % 3

    def couple(turn_number, carry):
        slot = order[turn_number]
        guest = jnp.maximum(slot - SLOTS, 0)
        for chunk in range(VERT // CHUNK):
            at = slice(chunk * CHUNK, (chunk + 1) * CHUNK)
            table = weights.at[chunk % 2]
            bead = moved[slot, :, at]
            along = [
                phi(jnp.broadcast_to(bead[k : k + 1, :], (8, CHUNK)) - step8) for k in range(3)
            ]
            along_x, along_y, along_z = along
            planes = [
                jnp.broadcast_to(along_z[iz : iz + 1, :], (8, CHUNK)) * along_x for iz in range(8)
            ]
            for iy in range(8):
                factor = jnp.broadcast_to(along_y[iy : iy + 1, :], (8, CHUNK))
                for pair in range(4):
                    both = jnp.concatenate(
                        [planes[2 * pair] * factor, planes[2 * pair + 1] * factor], axis=0
                    )
                    first = iy * 64 + pair * 16
                    table[first : first + 16, :] = both.astype(BF16)
            homes = []
            for b in range(CHUNK // 64):
                block = chunk * (CHUNK // 64) + b
                mine = bricks[0, 0, jnp.minimum(slot, SLOTS - 1), block]
                theirs = meta[guest // 2, 2 + guest % 2, block].astype(jnp.int32)
                homes.append(pl.multiple_of(jnp.where(slot < SLOTS, mine, theirs) * 8, 8))
            nearby = jnp.concatenate(
                [
                    jnp.concatenate([cells[j, pl.ds(home, 8), :] for j in range(4)], axis=1)
                    for home in homes
                ],
                axis=0,
            ).astype(BF16)
            drive = push[pl.ds(pl.multiple_of(slot * 8, 8), 8), at]
            drives = jnp.concatenate(
                [jnp.where(lane8 // 64 == b, drive, 0.0) for b in range(CHUNK // 64)], axis=0
            ).astype(BF16)
            sampled = jnp.dot(nearby, table[...], preferred_element_type=F32)
            spread = lax.dot_general(
                drives, table[...], (((1,), (1,)), ((), ())), preferred_element_type=F32
            )
            speed = sampled[0:8]
            for b in range(1, CHUNK // 64):
                speed = jnp.where(lane8 // 64 == b, sampled[8 * b : 8 * b + 8], speed)
            for b, home in enumerate(homes):
                for j in range(4):
                    force[j, pl.ds(home, 8), :] += spread[
                        8 * b : 8 * b + 8, 128 * j : 128 * j + 128
                    ]
            before = jnp.where(
                third == 0,
                jnp.broadcast_to(bead[6:7, :], (8, CHUNK)),
                jnp.where(
                    third == 1,
                    jnp.broadcast_to(bead[7:8, :], (8, CHUNK)),
                    jnp.broadcast_to(last[pl.ds(slot, 1), at], (8, CHUNK)),
                ),
            )
            vertex_out[0, 0, slot, 0:8, at] = jnp.where(
                row8 < 6, bead + 0.5 * (before + speed), speed
            )
            vertex_out[0, 0, slot, 8:9, at] = speed[2:3, :]
        return carry

    lax.fori_loop(0, count, couple, 0)

    for k in range(3):
        for bz in range(2):
            for j in range(4):
                base = bz * 2 * 16 * 8 + 3 + k
                zero = force[j, pl.ds(base, 16, stride=8), :]
                one = force[j, pl.ds(base + 128, 16, stride=8), :]
                turn[pl.ds(2 * j, 16, stride=8), :] = jnp.where(left, zero, pltpu.roll(one, 64, 1))
                turn[pl.ds(2 * j + 1, 16, stride=8), :] = jnp.where(
                    left, pltpu.roll(zero, 64, 1), one
                )
            back = turn[...].T
            for bx in range(2):
                for iz in range(8):
                    first = (8 * bz + iz) * CX + 8 * bx
                    flow[4 + k, first : first + 8, :] = back[(bx * 8 + iz) * 8 : (bx * 8 + iz) * 8 + 8]

    def collide(z, carry):
        at = pl.ds(pl.multiple_of(z * CX, CX), CX)
        density = flow[0, at, :]
        inverse = 1.0 / density
        body = [flow[4 + k, at, :] for k in range(3)]
        speed = [(flow[1 + k, at, :] + 0.5 * body[k]) * inverse for k in range(3)]
        square = speed[0] * speed[0] + speed[1] * speed[1] + speed[2] * speed[2]
        work = speed[0] * body[0] + speed[1] * body[1] + speed[2] * body[2]
        common = density * (1.25 - 1.875 * square) - 1.125 * work
        wall = solid[at, :] == 1
        read[0, at, :] = jnp.where(wall, read[0, at, :], WEIGHTS[0] * common - 0.25 * read[0, at, :])
        steep = 5.625 * density
        slope = 3.75 * density
        for q in range(1, 19, 2):
            along, push_along = None, None
            for c, s, b in zip(LATTICE[q], speed, body):
                if c != 0:
                    s, b = (s, b) if c > 0 else (-s, -b)
                    along = s if along is None else along + s
                    push_along = b if push_along is None else push_along + b
            even = WEIGHTS[q] * (common + along * (steep * along + 3.375 * push_along))
            odd = WEIGHTS[q] * (slope * along + 1.125 * push_along)
            here, there = read[q, at, :], read[q + 1, at, :]
            read[q, at, :] = jnp.where(wall, there, even + odd - 0.25 * here)
            read[q + 1, at, :] = jnp.where(wall, here, even - odd - 0.25 * there)
        return carry

    def ship(part):
        span = slice(part * 64, (part + 1) * 64)
        return pltpu.make_async_copy(
            read.at[:, span, :], pops_out.at[:, span, :], out_sem.at[part]
        )

    for part in range(4):
        lax.fori_loop(part * 4, part * 4 + 4, collide, 0)
        ship(part).start()
    for part in range(4):
        ship(part).wait()


def step(leave, bricks, pops, solid, states, faces, corners, stiffness):
    vmem = pl.BlockSpec(memory_space=pltpu.VMEM)
    smem = pl.BlockSpec(memory_space=pltpu.SMEM)
    hbm = pl.BlockSpec(memory_space=pl.ANY)
    return pl.pallas_call(
        step_kernel,
        out_shape=[
            jax.ShapeDtypeStruct((19, NZ * CX, CY), F32),
            jax.ShapeDtypeStruct((1, 1, ALL, 9, VERT), F32),
        ],
        in_specs=[smem, smem] + [vmem] * 12,
        out_specs=[hbm, vmem],
        scratch_shapes=[
            pltpu.VMEM((19, NZ * CX, CY), F32),
            pltpu.VMEM((7, NZ * CX, CY), F32),
            pltpu.VMEM((10, NZ, CY), F32),
            pltpu.VMEM((10, CX, CY), F32),
            pltpu.VMEM((128, 128), F32),
            pltpu.VMEM((4, 512, 128), F32),
            pltpu.VMEM((4, 512, 128), F32),
            pltpu.VMEM((ALL, 8, VERT), F32),
            pltpu.VMEM((ALL, VERT), F32),
            pltpu.VMEM((ALL * 8, VERT), F32),
            pltpu.VMEM((2, 512, CHUNK), BF16),
            pltpu.SMEM((4, 8, 128), F32),
            pltpu.SMEM((ALL + 1,), jnp.int32),
            pltpu.SemaphoreType.DMA((4,)),
            pltpu.SemaphoreType.DMA((4,)),
        ],
        compiler_params=pltpu.CompilerParams(vmem_limit_bytes=48 << 20),
        name="lattice_step",
    )(leave, bricks, pops, solid, states, *faces, *corners, stiffness)


def along_axis(x, axis, by):
    size = lax.axis_size(axis)
    return lax.ppermute(x, axis, [(i, (i + by) % size) for i in range(size)])


def across(x, dx, dy):
    nx, ny = lax.axis_size("gx"), lax.axis_size("gy")
    pairs = [
        (a * ny + b, (a + dx) % nx * ny + (b + dy) % ny) for a in range(nx) for b in range(ny)
    ]
    return lax.ppermute(x, ("gx", "gy"), pairs)


def local(populations, solid_mask, bead_states, bead_bricks, leave_dir, stiffness):
    pops = populations.reshape(19, NZ * CX, CY)
    solid = solid_mask.reshape(NZ * CX, CY)
    packed = pack(leave_dir, bead_bricks, pops, bead_states)
    faces = [
        along_axis(packed[0], "gx", 1),
        along_axis(packed[1], "gx", -1),
        along_axis(packed[2], "gy", 1),
        along_axis(packed[3], "gy", -1),
    ]
    corners = [across(x, dx, dy) for x, (_, dx, dy) in zip(packed[4:], CORNERS)]
    pops_out, vertex_out = step(
        leave_dir, bead_bricks, pops, solid, bead_states, faces, corners, stiffness
    )
    return (pops_out.reshape(populations.shape), vertex_out)


def solution(mesh):
    return jax.shard_map(
        local,
        mesh=mesh,
        in_specs=(
            P(None, None, "gx", "gy"),
            P(None, "gx", "gy"),
            P("gx", "gy", None, None, None),
            P("gx", "gy", None, None),
            P("gx", "gy", None),
            P(),
        ),
        out_specs=(P(None, None, "gx", "gy"), P("gx", "gy", None, None, None)),
        check_vma=False,
    )
```

```python
import functools

import jax
import jax.numpy as jnp
import numpy as np
from jax import lax
from jax.experimental import pallas as pl
from jax.experimental.pallas import tpu as pltpu
from jax.sharding import PartitionSpec as P

LATTICE = [
    (0, 0, 0),
    (1, 0, 0),
    (-1, 0, 0),
    (0, 1, 0),
    (0, -1, 0),
    (0, 0, 1),
    (0, 0, -1),
    (1, 1, 0),
    (-1, -1, 0),
    (1, -1, 0),
    (-1, 1, 0),
    (1, 0, 1),
    (-1, 0, -1),
    (1, 0, -1),
    (-1, 0, 1),
    (0, 1, 1),
    (0, -1, -1),
    (0, 1, -1),
    (0, -1, 1),
]
WEIGHTS = [1.0 / 3.0] + [1.0 / 18.0] * 6 + [1.0 / 36.0] * 12
X_UP = [1, 7, 9, 11, 13]
X_DOWN = [2, 8, 10, 12, 14]
Y_UP = [3, 7, 10, 15, 17]
Y_DOWN = [4, 8, 9, 16, 18]
NZ, CX, CY = 16, 16, 128
SLOTS, SIDES, MIG, ALL = 8, 4, 2, 16
VERT, BLOCKS, CHUNK = 1280, 20, 256
F32, BF16 = jnp.float32, jnp.bfloat16


def lanes(shape):
    return lax.broadcasted_iota(jnp.int32, shape, len(shape) - 1)


def rows(shape):
    return lax.broadcasted_iota(jnp.int32, shape, len(shape) - 2)


BEAD_ROWS, FLAG_ROWS, FACE_ROWS = 180, 180, 184
X_ROWS, Y_ROWS = FACE_ROWS + 5 * NZ, FACE_ROWS + CX


def pick(leave, code):
    first, second, count = jnp.int32(0), jnp.int32(0), jnp.int32(0)
    for slot in range(SLOTS):
        hit = leave[0, 0, slot] == code
        first = jnp.where(hit & (count == 0), slot, first)
        second = jnp.where(hit & (count == 1), slot, second)
        count = count + hit.astype(jnp.int32)
    return (first, second), count


def pack_beads(out, code, leave, bricks, states):
    chosen, count = pick(leave, code)
    out[176:184, :] = jnp.zeros((8, 128), F32)
    for place, slot in enumerate(chosen):
        for entry in range(9):
            row = states[entry, pl.ds(slot, 1), :]
            for c in range(VERT // 128):
                at = 18 * c + 2 * entry + place
                out[at : at + 1, :] = row[:, 128 * c : 128 * c + 128]
        valid = (count > place).astype(F32)
        at = FLAG_ROWS + place
        out[at : at + 1, :] = jnp.full((1, 128), 1.0, F32) * valid
        out[at : at + 1, 0:BLOCKS] = bricks[pl.ds(slot, 1), :].astype(F32)


def fetch_beads(leave_hbm, bricks_hbm, states_hbm, leave, bricks, states, sem):
    return [
        pltpu.make_async_copy(leave_hbm, leave, sem.at[0]),
        pltpu.make_async_copy(bricks_hbm.at[0, 0], bricks, sem.at[1]),
        pltpu.make_async_copy(states_hbm.at[0, 0], states, sem.at[2]),
    ]


def pack_x_kernel(
    leave_hbm, bricks_hbm, states_hbm, pops_hbm, up, down, leave, bricks, states, sem, face_sem
):
    copies = fetch_beads(leave_hbm, bricks_hbm, states_hbm, leave, bricks, states, sem)
    for side, (out, group, x) in enumerate(((up, X_UP, CX - 1), (down, X_DOWN, 0))):
        for i, q in enumerate(group):
            at = FACE_ROWS + NZ * i
            copies.append(
                pltpu.make_async_copy(
                    pops_hbm.at[q, :, x, :], out.at[at : at + NZ, :], face_sem.at[side * 5 + i]
                )
            )
    for copy in copies:
        copy.start()
    for copy in copies[:3]:
        copy.wait()
    pack_beads(up, 1, leave, bricks, states)
    pack_beads(down, 2, leave, bricks, states)
    for copy in copies[3:]:
        copy.wait()


Y_RANGES = ((3, 5), (7, 11), (15, 19))
Y_PLACE = {q: n for n, q in enumerate(q for lo, hi in Y_RANGES for q in range(lo, hi))}


def pack_y_kernel(
    leave_hbm, bricks_hbm, states_hbm, pops_hbm, up, down,
    leave, bricks, states, pops, sem, pops_sem,
):
    copies = fetch_beads(leave_hbm, bricks_hbm, states_hbm, leave, bricks, states, sem)
    for n, (lo, hi) in enumerate(Y_RANGES):
        at = Y_PLACE[lo]
        copies.append(
            pltpu.make_async_copy(
                pops_hbm.at[lo:hi], pops.at[at : at + hi - lo], pops_sem.at[n]
            )
        )
    for copy in copies:
        copy.start()
    for copy in copies[:3]:
        copy.wait()
    pack_beads(up, 3, leave, bricks, states)
    pack_beads(down, 4, leave, bricks, states)
    for copy in copies[3:]:
        copy.wait()
    lane = lanes((CX, CY))
    for out, group, y in ((up, Y_UP, CY - 1), (down, Y_DOWN, 0)):
        column = jnp.zeros((CX, CY), F32)
        for i, q in enumerate(group):
            for z in range(NZ):
                place = i * NZ + z
                column = jnp.where(
                    lane == place, pltpu.roll(pops[Y_PLACE[q], z], (place - y) % CY, 1), column
                )
        out[FACE_ROWS : FACE_ROWS + CX, :] = column


EDGES_UP = ((7, 0), (10, 1))
EDGES_DOWN = ((9, 0), (8, 1))


def edge_kernel(up, down, x_low, x_high, up_out, down_out):
    lane = lanes((NZ, CY))
    for source, out, edges, y in ((up, up_out, EDGES_UP, CY - 1), (down, down_out, EDGES_DOWN, 0)):
        out[0:FACE_ROWS, :] = source[0:FACE_ROWS, :]
        column = source[FACE_ROWS : FACE_ROWS + CX, :]
        for n, (q, side) in enumerate(edges):
            group, message = ((X_UP, x_low), (X_DOWN, x_high))[side]
            at = FACE_ROWS + NZ * group.index(q)
            moved = pltpu.roll(message[at : at + NZ, :], (80 + n - y) % CY, 1)
            column = jnp.where(lane == 80 + n, moved, column)
        out[FACE_ROWS : FACE_ROWS + CX, :] = column


VMEM = pl.BlockSpec(memory_space=pltpu.VMEM)
HBM = pl.BlockSpec(memory_space=pltpu.HBM)
BEAD_SCRATCH = [
    pltpu.SMEM((1, 1, SLOTS), jnp.int32),
    pltpu.VMEM((SLOTS, BLOCKS), jnp.int32),
    pltpu.VMEM((9, SLOTS, VERT), F32),
]


def pack_x(leave, bricks, states, pops):
    return pl.pallas_call(
        pack_x_kernel,
        out_shape=[jax.ShapeDtypeStruct((X_ROWS, 128), F32)] * 2,
        in_specs=[HBM] * 4,
        out_specs=[VMEM] * 2,
        scratch_shapes=BEAD_SCRATCH
        + [pltpu.SemaphoreType.DMA((3,)), pltpu.SemaphoreType.DMA((10,))],
        compiler_params=pltpu.CompilerParams(vmem_limit_bytes=60 << 20),
        cost_estimate=pl.CostEstimate(flops=10**6, bytes_accessed=10**6, transcendentals=0),
        name="pack_x",
    )(leave, bricks, states, pops)


def pack_y(leave, bricks, states, pops):
    return pl.pallas_call(
        pack_y_kernel,
        out_shape=[jax.ShapeDtypeStruct((Y_ROWS, 128), F32)] * 2,
        in_specs=[HBM] * 4,
        out_specs=[VMEM] * 2,
        scratch_shapes=BEAD_SCRATCH
        + [
            pltpu.VMEM((10, NZ, CX, CY), F32),
            pltpu.SemaphoreType.DMA((3,)),
            pltpu.SemaphoreType.DMA((3,)),
        ],
        compiler_params=pltpu.CompilerParams(vmem_limit_bytes=8 << 20),
        cost_estimate=pl.CostEstimate(flops=10**6, bytes_accessed=2 * 10**6, transcendentals=0),
        name="pack_y",
    )(leave, bricks, states, pops)


def add_edges(up, down, x_low, x_high):
    return pl.pallas_call(
        edge_kernel,
        out_shape=[jax.ShapeDtypeStruct((Y_ROWS, 128), F32)] * 2,
        in_specs=[VMEM] * 4,
        out_specs=[VMEM] * 2,
        compiler_params=pltpu.CompilerParams(vmem_limit_bytes=8 << 20),
        name="add_edges",
    )(up, down, x_low, x_high)


def phi(distance):
    t = distance * distance
    value = jnp.full(t.shape, COSINE[-1], F32)
    for coefficient in COSINE[-2::-1]:
        value = value * t + coefficient
    return jnp.where(jnp.abs(distance) < 2.0, 0.5 * (value * value), 0.0)


def cosine_terms():
    terms, term = [], 1.0
    for n in range(8):
        terms.append(float(term))
        term = -term * (np.pi / 4) ** 2 / ((2 * n + 1) * (2 * n + 2))
    return terms


COSINE = cosine_terms()
PER_CHUNK = CHUNK // 64


def fill_table(table, states, slot, at):
    step8 = rows((8, CHUNK)).astype(F32)
    along_x, along_y, along_z = [
        phi(jnp.broadcast_to(states[k, pl.ds(slot, 1), at], (8, CHUNK)) - step8) for k in range(3)
    ]
    planes = [jnp.broadcast_to(along_z[iz : iz + 1, :], (8, CHUNK)) * along_x for iz in range(8)]
    for iy in range(8):
        factor = jnp.broadcast_to(along_y[iy : iy + 1, :], (8, CHUNK))
        for pair in range(4):
            both = jnp.concatenate(
                [planes[2 * pair] * factor, planes[2 * pair + 1] * factor], axis=0
            )
            first = iy * 64 + pair * 16
            table[first : first + 16, :] = both.astype(BF16)


def stiff_product(push, states, stiffness):
    shape = states[3:6].reshape(24, VERT).astype(BF16)
    for n in range(5):
        at = slice(n * 256, (n + 1) * 256)
        push[:, at] = -jnp.dot(shape, stiffness[:, at], preferred_element_type=F32)


def spread_chunk(force, table, push, slot, at, homes):
    row8 = rows((8, CHUNK))
    block = lanes((8, CHUNK)) // 64
    parts = [
        jnp.broadcast_to(push[pl.ds(8 * k + slot, 1), at], (8, CHUNK)) for k in range(3)
    ]
    drive = jnp.where(row8 == 0, parts[0], jnp.where(row8 == 1, parts[1], parts[2]))
    drives = jnp.concatenate(
        [jnp.where(block == b, drive, 0.0) for b in range(PER_CHUNK)], axis=0
    ).astype(BF16)
    spread = lax.dot_general(
        drives, table[...], (((1,), (1,)), ((), ())), preferred_element_type=F32
    )
    for b, home in enumerate(homes):
        for j in range(4):
            force[j, pl.ds(home, 8), :] += spread[8 * b : 8 * b + 8, 128 * j : 128 * j + 128]


def sample_chunk(sampled_speed, cells, table, slot, at, homes):
    block = lanes((8, CHUNK)) // 64
    nearby = jnp.concatenate(
        [
            jnp.concatenate([cells[j, pl.ds(home, 8), :] for j in range(4)], axis=1)
            for home in homes
        ],
        axis=0,
    ).astype(BF16)
    sampled = jnp.dot(nearby, table[...], preferred_element_type=F32)
    speed = sampled[0:8]
    for b in range(1, PER_CHUNK):
        speed = jnp.where(block == b, sampled[8 * b : 8 * b + 8], speed)
    for k in range(3):
        sampled_speed[k, pl.ds(slot, 1), at] = speed[k : k + 1, :]


def list_active(order, flags):
    count = jnp.int32(0)
    for slot, flag in enumerate(flags):
        order[count] = slot
        count = count + flag.astype(jnp.int32)
    return count


def own_kernel(
    leave_hbm, bricks_hbm, states, stiffness, force, leave, bricks, push, tables, order, sem
):
    copies = [
        pltpu.make_async_copy(leave_hbm, leave, sem.at[0]),
        pltpu.make_async_copy(bricks_hbm, bricks, sem.at[1]),
    ]
    for copy in copies:
        copy.start()
    stiff_product(push, states.at[0, 0], stiffness)
    force[...] = jnp.zeros(force.shape, F32)
    for copy in copies:
        copy.wait()
    count = list_active(order, [leave[0, 0, slot] == 0 for slot in range(SLOTS)])

    def couple(turn_number, carry):
        slot = order[turn_number]
        for chunk in range(VERT // CHUNK):
            at = slice(chunk * CHUNK, (chunk + 1) * CHUNK)
            table = tables.at[chunk % 2]
            fill_table(table, states.at[0, 0], slot, at)
            homes = [
                pl.multiple_of(bricks[0, 0, slot, chunk * PER_CHUNK + b] * 8, 8)
                for b in range(PER_CHUNK)
            ]
            spread_chunk(force, table, push, slot, at, homes)
        return carry

    lax.fori_loop(0, count, couple, 0)


def spread_own(leave, bricks, states, stiffness):
    return pl.pallas_call(
        own_kernel,
        out_shape=jax.ShapeDtypeStruct((4, 512, 128), F32),
        in_specs=[HBM, HBM, VMEM, VMEM],
        out_specs=VMEM,
        scratch_shapes=[
            pltpu.SMEM((1, 1, SLOTS), jnp.int32),
            pltpu.SMEM((1, 1, SLOTS, BLOCKS), jnp.int32),
            pltpu.VMEM((24, VERT), F32),
            pltpu.VMEM((2, 512, CHUNK), BF16),
            pltpu.SMEM((SLOTS + 1,), jnp.int32),
            pltpu.SemaphoreType.DMA((2,)),
        ],
        compiler_params=pltpu.CompilerParams(vmem_limit_bytes=16 << 20),
        cost_estimate=pl.CostEstimate(
            flops=2 * 10**9, bytes_accessed=5 * 10**6, transcendentals=0
        ),
        name="spread_own",
    )(leave, bricks, states, stiffness)


def step_kernel(
    leave_hbm, bricks_hbm, pops, solid, states_in, own_force,
    x_low, x_high, y_low, y_high,
    stiffness,
    pops_out, vertex_out,
    read, flow, halo_y, turn, cells, force, guests, push, tables, speeds, vertex,
    leave, bricks, meta, order, meta_sem, out_sem,
):
    faces = (x_low, x_high, y_low, y_high)
    states = states_in.at[0, 0]
    copies = [
        pltpu.make_async_copy(faces[side].at[176:184, :], meta.at[side], meta_sem.at[side])
        for side in range(4)
    ] + [
        pltpu.make_async_copy(leave_hbm, leave, meta_sem.at[4]),
        pltpu.make_async_copy(bricks_hbm, bricks, meta_sem.at[5]),
    ]
    for copy in copies:
        copy.start()

    for side in range(4):
        for c in range(VERT // 128):
            for entry in range(9):
                guests[entry, 2 * side : 2 * side + 2, 128 * c : 128 * c + 128] = faces[side][
                    18 * c + 2 * entry : 18 * c + 2 * entry + 2, :
                ]

    row16 = rows((CX, CY))
    lane16 = lanes((CX, CY))
    for side, group in enumerate((Y_UP, Y_DOWN)):
        column = faces[2 + side][FACE_ROWS : FACE_ROWS + CX, :]
        for i, q in enumerate(group):
            cx = LATTICE[q][0]
            halo_y[side * 5 + i] = column if cx == 0 else pltpu.roll(column, cx % CX, 0)

    def pull(z, carry):
        density = None
        momentum = [None, None, None]
        at = pl.ds(pl.multiple_of(z * CX, CX), CX)
        for q in range(19):
            cx, cy, cz = LATTICE[q]
            source = (z - cz) & (NZ - 1)
            value = pops[q, pl.ds(pl.multiple_of(source * CX, CX), CX), :]
            if cx != 0:
                x = 0 if cx > 0 else CX - 1
                side, group = (0, X_UP) if cx > 0 else (1, X_DOWN)
                edge = faces[side][pl.ds(FACE_ROWS + NZ * group.index(q) + source, 1), :]
                value = jnp.where(
                    row16 == x, jnp.broadcast_to(edge, (CX, CY)), pltpu.roll(value, cx % CX, 0)
                )
            if cy != 0:
                side, group, edges = (0, Y_UP, EDGES_UP) if cy > 0 else (1, Y_DOWN, EDGES_DOWN)
                i = group.index(q)
                y = 0 if cy > 0 else CY - 1
                column = pltpu.roll(
                    halo_y[side * 5 + i], (y + 2 * CY - i * NZ - source) & (CY - 1), 1
                )
                if cx != 0:
                    n = [e[0] for e in edges].index(q)
                    corner = faces[2 + side][pl.ds(FACE_ROWS + source, 1), :]
                    corner = pltpu.roll(jnp.broadcast_to(corner, (CX, CY)), (y - 80 - n) % CY, 1)
                    column = jnp.where(row16 == x, corner, column)
                value = jnp.where(lane16 == y, column, pltpu.roll(value, cy % CY, 1))
            read[q, at, :] = value
            density = value if density is None else density + value
            for k, c in enumerate((cx, cy, cz)):
                if c != 0:
                    signed = value if c > 0 else -value
                    momentum[k] = signed if momentum[k] is None else momentum[k] + signed
        inverse = 1.0 / density
        flow[0, at, :] = density
        for k in range(3):
            flow[1 + k, at, :] = momentum[k]
            flow[4 + k, at, :] = momentum[k] * inverse
        return carry

    lax.fori_loop(0, NZ, pull, 0)

    left = lanes((16, 128)) < 64
    for k in range(3):
        for bz in range(2):
            tiles = [
                flow[4 + k, (8 * bz + iz) * CX + 8 * bx : (8 * bz + iz) * CX + 8 * bx + 8, :]
                for bx in range(2)
                for iz in range(8)
            ]
            turn[...] = jnp.concatenate(tiles, axis=0).T
            for j in range(4):
                even = turn[pl.ds(2 * j, 16, stride=8), :]
                odd = turn[pl.ds(2 * j + 1, 16, stride=8), :]
                pairs = (
                    jnp.where(left, even, pltpu.roll(odd, 64, 1)),
                    jnp.where(left, pltpu.roll(even, 64, 1), odd),
                )
                for bx in range(2):
                    base = (bz * 2 + bx) * 16 * 8
                    cells[j, pl.ds(base + k, 16, stride=8), :] = pairs[bx]

    stiff_product(push, guests, stiffness)
    force[...] = jnp.zeros(force.shape, F32)
    speeds[...] = jnp.zeros(speeds.shape, F32)
    for copy in copies:
        copy.wait()

    def sample_own(turn_number, carry):
        slot = order[turn_number]
        for chunk in range(VERT // CHUNK):
            at = slice(chunk * CHUNK, (chunk + 1) * CHUNK)
            table = tables.at[chunk % 2]
            fill_table(table, states, slot, at)
            homes = [
                pl.multiple_of(bricks[0, 0, slot, chunk * PER_CHUNK + b] * 8, 8)
                for b in range(PER_CHUNK)
            ]
            sample_chunk(speeds.at[0], cells, table, slot, at, homes)
        return carry

    def couple_guest(turn_number, carry):
        slot = order[turn_number]
        for chunk in range(VERT // CHUNK):
            at = slice(chunk * CHUNK, (chunk + 1) * CHUNK)
            table = tables.at[chunk % 2]
            fill_table(table, guests, slot, at)
            homes = [
                pl.multiple_of(
                    meta[slot // 2, 4 + slot % 2, chunk * PER_CHUNK + b].astype(jnp.int32) * 8, 8
                )
                for b in range(PER_CHUNK)
            ]
            sample_chunk(speeds.at[1], cells, table, slot, at, homes)
            spread_chunk(force, table, push, slot, at, homes)
        return carry

    stays = [leave[0, 0, slot] == 0 for slot in range(SLOTS)]
    lax.fori_loop(0, list_active(order, stays), sample_own, 0)
    arrives = [meta[slot // 2, 4 + slot % 2, 64] > 0.5 for slot in range(SLOTS)]
    lax.fori_loop(0, list_active(order, arrives), couple_guest, 0)

    row8 = rows((8, VERT))
    for part, (source, flags) in enumerate(((states, stays), (guests, arrives))):
        active = jnp.zeros((8, VERT), jnp.int32)
        for slot, flag in enumerate(flags):
            active = jnp.where(row8 == slot, flag.astype(jnp.int32), active)
        span = slice(8 * part, 8 * part + 8)
        for k in range(3):
            speed = speeds[part, k]
            half = 0.5 * (source[6 + k] + speed)
            vertex[k, span, :] = jnp.where(active == 1, source[k] + half, 0.0)
            vertex[3 + k, span, :] = jnp.where(active == 1, source[3 + k] + half, 0.0)
            vertex[6 + k, span, :] = jnp.where(active == 1, speed, 0.0)
    vertex_copy = pltpu.make_async_copy(vertex, vertex_out.at[0, 0], out_sem.at[4])
    vertex_copy.start()

    for k in range(3):
        for bz in range(2):
            for j in range(4):
                base = bz * 2 * 16 * 8 + k
                zero = pl.ds(base, 16, stride=8)
                one = pl.ds(base + 128, 16, stride=8)
                zero = force[j, zero, :] + own_force[j, zero, :]
                one = force[j, one, :] + own_force[j, one, :]
                turn[pl.ds(2 * j, 16, stride=8), :] = jnp.where(left, zero, pltpu.roll(one, 64, 1))
                turn[pl.ds(2 * j + 1, 16, stride=8), :] = jnp.where(
                    left, pltpu.roll(zero, 64, 1), one
                )
            back = turn[...].T
            for bx in range(2):
                for iz in range(8):
                    first = (8 * bz + iz) * CX + 8 * bx
                    flow[4 + k, first : first + 8, :] = back[(bx * 8 + iz) * 8 : (bx * 8 + iz) * 8 + 8]

    def collide(z, carry):
        at = pl.ds(pl.multiple_of(z * CX, CX), CX)
        density = flow[0, at, :]
        inverse = 1.0 / density
        body = [flow[4 + k, at, :] for k in range(3)]
        speed = [(flow[1 + k, at, :] + 0.5 * body[k]) * inverse for k in range(3)]
        square = speed[0] * speed[0] + speed[1] * speed[1] + speed[2] * speed[2]
        work = speed[0] * body[0] + speed[1] * body[1] + speed[2] * body[2]
        common = density * (1.25 - 1.875 * square) - 1.125 * work
        wall = solid[at, :] == 1
        read[0, at, :] = jnp.where(wall, read[0, at, :], WEIGHTS[0] * common - 0.25 * read[0, at, :])
        steep = 5.625 * density
        slope = 3.75 * density
        for q in range(1, 19, 2):
            along, push_along = None, None
            for c, s, b in zip(LATTICE[q], speed, body):
                if c != 0:
                    s, b = (s, b) if c > 0 else (-s, -b)
                    along = s if along is None else along + s
                    push_along = b if push_along is None else push_along + b
            even = WEIGHTS[q] * (common + along * (steep * along + 3.375 * push_along))
            odd = WEIGHTS[q] * (slope * along + 1.125 * push_along)
            here, there = read[q, at, :], read[q + 1, at, :]
            read[q, at, :] = jnp.where(wall, there, even + odd - 0.25 * here)
            read[q + 1, at, :] = jnp.where(wall, here, even - odd - 0.25 * there)
        return carry

    def ship(part):
        span = slice(part * 64, (part + 1) * 64)
        return pltpu.make_async_copy(
            read.at[:, span, :], pops_out.at[:, span, :], out_sem.at[part]
        )

    for part in range(4):
        lax.fori_loop(part * 4, part * 4 + 4, collide, 0)
        ship(part).start()
    vertex_copy.wait()
    for part in range(4):
        ship(part).wait()


def step(leave, bricks, pops, solid, states, own_force, faces, stiffness):
    return pl.pallas_call(
        step_kernel,
        out_shape=[
            jax.ShapeDtypeStruct((19, NZ * CX, CY), F32),
            jax.ShapeDtypeStruct((1, 1, 9, ALL, VERT), F32),
        ],
        in_specs=[HBM, HBM] + [VMEM] * 9,
        out_specs=[HBM, HBM],
        scratch_shapes=[
            pltpu.VMEM((19, NZ * CX, CY), F32),
            pltpu.VMEM((7, NZ * CX, CY), F32),
            pltpu.VMEM((10, CX, CY), F32),
            pltpu.VMEM((128, 128), F32),
            pltpu.VMEM((4, 512, 128), F32),
            pltpu.VMEM((4, 512, 128), F32),
            pltpu.VMEM((9, SLOTS, VERT), F32),
            pltpu.VMEM((24, VERT), F32),
            pltpu.VMEM((2, 512, CHUNK), BF16),
            pltpu.VMEM((2, 3, SLOTS, VERT), F32),
            pltpu.VMEM((9, ALL, VERT), F32),
            pltpu.SMEM((1, 1, SLOTS), jnp.int32),
            pltpu.SMEM((1, 1, SLOTS, BLOCKS), jnp.int32),
            pltpu.SMEM((4, 8, 128), F32),
            pltpu.SMEM((SLOTS + 1,), jnp.int32),
            pltpu.SemaphoreType.DMA((6,)),
            pltpu.SemaphoreType.DMA((5,)),
        ],
        compiler_params=pltpu.CompilerParams(vmem_limit_bytes=24 << 20),
        cost_estimate=pl.CostEstimate(
            flops=2 * 10**9, bytes_accessed=10**7, transcendentals=0
        ),
        name="lattice_step",
    )(leave, bricks, pops, solid, states, own_force, *faces, stiffness)


def along_axis(x, axis, by):
    size = lax.axis_size(axis)
    return lax.ppermute(x, axis, [(i, (i + by) % size) for i in range(size)])


def local(populations, solid_mask, bead_states, bead_bricks, leave_dir, stiffness):
    pops = populations.reshape(19, NZ * CX, CY)
    solid = solid_mask.reshape(NZ * CX, CY)
    states = bead_states.transpose(0, 1, 3, 2, 4)
    x_up, x_down = pack_x(leave_dir, bead_bricks, states, populations)
    x_low = along_axis(x_up, "gx", 1)
    x_high = along_axis(x_down, "gx", -1)
    y_up, y_down = pack_y(leave_dir, bead_bricks, states, populations)
    y_up, y_down = add_edges(y_up, y_down, x_low, x_high)
    y_low = along_axis(y_up, "gy", 1)
    y_high = along_axis(y_down, "gy", -1)
    own_force = spread_own(leave_dir, bead_bricks, states, stiffness)
    pops_out, vertex_out = step(
        leave_dir, bead_bricks, pops, solid, states, own_force,
        (x_low, x_high, y_low, y_high), stiffness,
    )
    return (pops_out.reshape(populations.shape), vertex_out.transpose(0, 1, 3, 2, 4))


def solution(mesh):
    return jax.shard_map(
        local,
        mesh=mesh,
        in_specs=(
            P(None, None, "gx", "gy"),
            P(None, "gx", "gy"),
            P("gx", "gy", None, None, None),
            P("gx", "gy", None, None),
            P("gx", "gy", None),
            P(),
        ),
        out_specs=(P(None, None, "gx", "gy"), P("gx", "gy", None, None, None)),
        check_vma=False,
    )
```

```python
import functools

import jax
import jax.numpy as jnp
import numpy as np
from jax import lax
from jax.experimental import pallas as pl
from jax.experimental.pallas import tpu as pltpu
from jax.sharding import PartitionSpec as P

LATTICE = [
    (0, 0, 0),
    (1, 0, 0),
    (-1, 0, 0),
    (0, 1, 0),
    (0, -1, 0),
    (0, 0, 1),
    (0, 0, -1),
    (1, 1, 0),
    (-1, -1, 0),
    (1, -1, 0),
    (-1, 1, 0),
    (1, 0, 1),
    (-1, 0, -1),
    (1, 0, -1),
    (-1, 0, 1),
    (0, 1, 1),
    (0, -1, -1),
    (0, 1, -1),
    (0, -1, 1),
]
WEIGHTS = [1.0 / 3.0] + [1.0 / 18.0] * 6 + [1.0 / 36.0] * 12
X_UP = [1, 7, 9, 11, 13]
X_DOWN = [2, 8, 10, 12, 14]
Y_UP = [3, 7, 10, 15, 17]
Y_DOWN = [4, 8, 9, 16, 18]
NZ, CX, CY = 16, 16, 128
SLOTS, SIDES, MIG, ALL = 8, 4, 2, 16
VERT, BLOCKS, CHUNK = 1280, 20, 256
F32, BF16 = jnp.float32, jnp.bfloat16


def lanes(shape):
    return lax.broadcasted_iota(jnp.int32, shape, len(shape) - 1)


def rows(shape):
    return lax.broadcasted_iota(jnp.int32, shape, len(shape) - 2)


BEAD_ROWS, FLAG_ROWS, FACE_ROWS = 180, 180, 184
X_ROWS, Y_ROWS = FACE_ROWS + 5 * NZ, FACE_ROWS + CX


def parity(axis):
    return lax.axis_index(axis) & 1


def pick(leave, code):
    first, second, count = jnp.int32(0), jnp.int32(0), jnp.int32(0)
    for slot in range(SLOTS):
        hit = leave[0, 0, slot] == code
        first = jnp.where(hit & (count == 0), slot, first)
        second = jnp.where(hit & (count == 1), slot, second)
        count = count + hit.astype(jnp.int32)
    return (first, second), count


def pack_beads(out, code, leave, bricks, states):
    chosen, count = pick(leave, code)
    out[176:184, :] = jnp.zeros((8, 128), F32)
    for place, slot in enumerate(chosen):
        for entry in range(9):
            row = states[entry, pl.ds(slot, 1), :]
            for c in range(VERT // 128):
                at = 18 * c + 2 * entry + place
                out[at : at + 1, :] = row[:, 128 * c : 128 * c + 128]
        valid = (count > place).astype(F32)
        at = FLAG_ROWS + place
        out[at : at + 1, :] = jnp.full((1, 128), 1.0, F32) * valid
        out[at : at + 1, 0:BLOCKS] = bricks[pl.ds(slot, 1), :].astype(F32)


def fetch_beads(leave_hbm, bricks_hbm, states_hbm, leave, bricks, states, sem):
    return [
        pltpu.make_async_copy(leave_hbm, leave, sem.at[0]),
        pltpu.make_async_copy(bricks_hbm.at[0, 0], bricks, sem.at[1]),
        pltpu.make_async_copy(states_hbm.at[0, 0], states, sem.at[2]),
    ]


def pack_x_kernel(
    leave_hbm, bricks_hbm, states_hbm, pops_hbm, near, far, leave, bricks, states, sem, face_sem
):
    copies = fetch_beads(leave_hbm, bricks_hbm, states_hbm, leave, bricks, states, sem)
    near_down = parity("gx")
    for n, (out, down) in enumerate(((near, near_down), (far, 1 - near_down))):
        x = (1 - down) * (CX - 1)
        for i, q in enumerate(X_UP):
            at = FACE_ROWS + NZ * i
            copies.append(
                pltpu.make_async_copy(
                    pops_hbm.at[q + down, :, x, :], out.at[at : at + NZ, :], face_sem.at[n * 5 + i]
                )
            )
    for copy in copies:
        copy.start()
    for copy in copies[:3]:
        copy.wait()
    pack_beads(near, 1 + near_down, leave, bricks, states)
    pack_beads(far, 2 - near_down, leave, bricks, states)
    for copy in copies[3:]:
        copy.wait()


Y_RANGES = ((3, 5), (7, 11), (15, 19))
Y_PLACE = {q: n for n, q in enumerate(q for lo, hi in Y_RANGES for q in range(lo, hi))}


def pack_y_kernel(
    leave_hbm, bricks_hbm, states_hbm, pops_hbm, near, far,
    leave, bricks, states, pops, sem, pops_sem,
):
    copies = fetch_beads(leave_hbm, bricks_hbm, states_hbm, leave, bricks, states, sem)
    for n, (lo, hi) in enumerate(Y_RANGES):
        at = Y_PLACE[lo]
        copies.append(
            pltpu.make_async_copy(
                pops_hbm.at[lo:hi], pops.at[at : at + hi - lo], pops_sem.at[n]
            )
        )
    for copy in copies:
        copy.start()
    for copy in copies[:3]:
        copy.wait()
    near_down = parity("gy")
    pack_beads(near, 3 + near_down, leave, bricks, states)
    pack_beads(far, 4 - near_down, leave, bricks, states)
    for copy in copies[3:]:
        copy.wait()
    lane = lanes((CX, CY))
    columns = []
    for group, y in ((Y_UP, CY - 1), (Y_DOWN, 0)):
        column = jnp.zeros((CX, CY), F32)
        for i, q in enumerate(group):
            for z in range(NZ):
                place = i * NZ + z
                column = jnp.where(
                    lane == place, pltpu.roll(pops[Y_PLACE[q], z], (place - y) % CY, 1), column
                )
        columns.append(column)
    near[FACE_ROWS : FACE_ROWS + CX, :] = jnp.where(near_down == 1, columns[1], columns[0])
    far[FACE_ROWS : FACE_ROWS + CX, :] = jnp.where(near_down == 1, columns[0], columns[1])


EDGES_UP = ((7, 0), (10, 1))
EDGES_DOWN = ((9, 0), (8, 1))


def edge_kernel(y_near, y_far, x_near, x_far, near_out, far_out):
    lane = lanes((NZ, CY))
    low_is_near = parity("gx") == 1
    near_down = parity("gy") == 1
    extra = []
    for edges, y in ((EDGES_UP, CY - 1), (EDGES_DOWN, 0)):
        column = jnp.zeros((NZ, CY), F32)
        for n, (q, side) in enumerate(edges):
            at = FACE_ROWS + NZ * (X_UP, X_DOWN)[side].index(q)
            near, far = x_near[at : at + NZ, :], x_far[at : at + NZ, :]
            face = jnp.where(low_is_near, *((near, far) if side == 0 else (far, near)))
            column = jnp.where(lane == 80 + n, pltpu.roll(face, (80 + n - y) % CY, 1), column)
        extra.append(column)
    up, down = extra
    for source, out, add in (
        (y_near, near_out, jnp.where(near_down, down, up)),
        (y_far, far_out, jnp.where(near_down, up, down)),
    ):
        out[0:FACE_ROWS, :] = source[0:FACE_ROWS, :]
        column = source[FACE_ROWS : FACE_ROWS + CX, :]
        out[FACE_ROWS : FACE_ROWS + CX, :] = jnp.where(lane < 80, column, add)


VMEM = pl.BlockSpec(memory_space=pltpu.VMEM)
HBM = pl.BlockSpec(memory_space=pltpu.HBM)
BEAD_SCRATCH = [
    pltpu.SMEM((1, 1, SLOTS), jnp.int32),
    pltpu.VMEM((SLOTS, BLOCKS), jnp.int32),
    pltpu.VMEM((9, SLOTS, VERT), F32),
]


def pack_x(leave, bricks, states, pops):
    return pl.pallas_call(
        pack_x_kernel,
        out_shape=[jax.ShapeDtypeStruct((X_ROWS, 128), F32)] * 2,
        in_specs=[HBM] * 4,
        out_specs=[VMEM] * 2,
        scratch_shapes=BEAD_SCRATCH
        + [pltpu.SemaphoreType.DMA((3,)), pltpu.SemaphoreType.DMA((10,))],
        compiler_params=pltpu.CompilerParams(vmem_limit_bytes=60 << 20),
        cost_estimate=pl.CostEstimate(flops=10**6, bytes_accessed=10**6, transcendentals=0),
        name="pack_x",
    )(leave, bricks, states, pops)


def pack_y(leave, bricks, states, pops):
    return pl.pallas_call(
        pack_y_kernel,
        out_shape=[jax.ShapeDtypeStruct((Y_ROWS, 128), F32)] * 2,
        in_specs=[HBM] * 4,
        out_specs=[VMEM] * 2,
        scratch_shapes=BEAD_SCRATCH
        + [
            pltpu.VMEM((10, NZ, CX, CY), F32),
            pltpu.SemaphoreType.DMA((3,)),
            pltpu.SemaphoreType.DMA((3,)),
        ],
        compiler_params=pltpu.CompilerParams(vmem_limit_bytes=8 << 20),
        cost_estimate=pl.CostEstimate(flops=10**6, bytes_accessed=2 * 10**6, transcendentals=0),
        name="pack_y",
    )(leave, bricks, states, pops)


def add_edges(y_near, y_far, x_near, x_far):
    return pl.pallas_call(
        edge_kernel,
        out_shape=[jax.ShapeDtypeStruct((Y_ROWS, 128), F32)] * 2,
        in_specs=[VMEM] * 4,
        out_specs=[VMEM] * 2,
        compiler_params=pltpu.CompilerParams(vmem_limit_bytes=8 << 20),
        name="add_edges",
    )(y_near, y_far, x_near, x_far)


def phi(distance):
    t = distance * distance
    value = jnp.full(t.shape, COSINE[-1], F32)
    for coefficient in COSINE[-2::-1]:
        value = value * t + coefficient
    return jnp.where(jnp.abs(distance) < 2.0, 0.5 * (value * value), 0.0)


def cosine_terms():
    terms, term = [], 1.0
    for n in range(8):
        terms.append(float(term))
        term = -term * (np.pi / 4) ** 2 / ((2 * n + 1) * (2 * n + 2))
    return terms


COSINE = cosine_terms()
PER_CHUNK = CHUNK // 64


def fill_table(table, states, slot, at):
    step8 = rows((8, CHUNK)).astype(F32)
    along_x, along_y, along_z = [
        phi(jnp.broadcast_to(states[k, pl.ds(slot, 1), at], (8, CHUNK)) - step8) for k in range(3)
    ]
    planes = [jnp.broadcast_to(along_z[iz : iz + 1, :], (8, CHUNK)) * along_x for iz in range(8)]
    for iy in range(8):
        factor = jnp.broadcast_to(along_y[iy : iy + 1, :], (8, CHUNK))
        for pair in range(4):
            both = jnp.concatenate(
                [planes[2 * pair] * factor, planes[2 * pair + 1] * factor], axis=0
            )
            first = iy * 64 + pair * 16
            table[first : first + 16, :] = both.astype(BF16)


def stiff_product(push, states, stiffness):
    shape = states[3:6].reshape(24, VERT).astype(BF16)
    for n in range(5):
        at = slice(n * 256, (n + 1) * 256)
        push[:, at] = -jnp.dot(shape, stiffness[:, at], preferred_element_type=F32)


def spread_chunk(force, table, push, slot, at, homes):
    row8 = rows((8, CHUNK))
    block = lanes((8, CHUNK)) // 64
    parts = [
        jnp.broadcast_to(push[pl.ds(8 * k + slot, 1), at], (8, CHUNK)) for k in range(3)
    ]
    drive = jnp.where(row8 == 0, parts[0], jnp.where(row8 == 1, parts[1], parts[2]))
    drives = jnp.concatenate(
        [jnp.where(block == b, drive, 0.0) for b in range(PER_CHUNK)], axis=0
    ).astype(BF16)
    spread = lax.dot_general(
        drives, table[...], (((1,), (1,)), ((), ())), preferred_element_type=F32
    )
    for b, home in enumerate(homes):
        for j in range(4):
            force[j, pl.ds(home, 8), :] += spread[8 * b : 8 * b + 8, 128 * j : 128 * j + 128]


def sample_chunk(sampled_speed, cells, table, slot, at, homes):
    block = lanes((8, CHUNK)) // 64
    nearby = jnp.concatenate(
        [
            jnp.concatenate([cells[j, pl.ds(home, 8), :] for j in range(4)], axis=1)
            for home in homes
        ],
        axis=0,
    ).astype(BF16)
    sampled = jnp.dot(nearby, table[...], preferred_element_type=F32)
    speed = sampled[0:8]
    for b in range(1, PER_CHUNK):
        speed = jnp.where(block == b, sampled[8 * b : 8 * b + 8], speed)
    for k in range(3):
        sampled_speed[k, pl.ds(slot, 1), at] = speed[k : k + 1, :]


def list_active(order, flags):
    count = jnp.int32(0)
    for slot, flag in enumerate(flags):
        order[count] = slot
        count = count + flag.astype(jnp.int32)
    return count


def own_kernel(
    leave_hbm, bricks_hbm, states, stiffness, force, leave, bricks, push, tables, order, sem
):
    copies = [
        pltpu.make_async_copy(leave_hbm, leave, sem.at[0]),
        pltpu.make_async_copy(bricks_hbm, bricks, sem.at[1]),
    ]
    for copy in copies:
        copy.start()
    stiff_product(push, states.at[0, 0], stiffness)
    force[...] = jnp.zeros(force.shape, F32)
    for copy in copies:
        copy.wait()
    count = list_active(order, [leave[0, 0, slot] == 0 for slot in range(SLOTS)])

    def couple(turn_number, carry):
        slot = order[turn_number]
        for chunk in range(VERT // CHUNK):
            at = slice(chunk * CHUNK, (chunk + 1) * CHUNK)
            table = tables.at[chunk % 2]
            fill_table(table, states.at[0, 0], slot, at)
            homes = [
                pl.multiple_of(bricks[0, 0, slot, chunk * PER_CHUNK + b] * 8, 8)
                for b in range(PER_CHUNK)
            ]
            spread_chunk(force, table, push, slot, at, homes)
        return carry

    lax.fori_loop(0, count, couple, 0)


def spread_own(leave, bricks, states, stiffness):
    return pl.pallas_call(
        own_kernel,
        out_shape=jax.ShapeDtypeStruct((4, 512, 128), F32),
        in_specs=[HBM, HBM, VMEM, VMEM],
        out_specs=VMEM,
        scratch_shapes=[
            pltpu.SMEM((1, 1, SLOTS), jnp.int32),
            pltpu.SMEM((1, 1, SLOTS, BLOCKS), jnp.int32),
            pltpu.VMEM((24, VERT), F32),
            pltpu.VMEM((2, 512, CHUNK), BF16),
            pltpu.SMEM((SLOTS + 1,), jnp.int32),
            pltpu.SemaphoreType.DMA((2,)),
        ],
        compiler_params=pltpu.CompilerParams(vmem_limit_bytes=16 << 20),
        cost_estimate=pl.CostEstimate(
            flops=2 * 10**9, bytes_accessed=5 * 10**6, transcendentals=0
        ),
        name="spread_own",
    )(leave, bricks, states, stiffness)


def step_kernel(
    leave_hbm, bricks_hbm, pops, solid, states_in, own_force,
    x_near, x_far, y_near, y_far,
    stiffness,
    pops_out, vertex_out,
    read, flow, halo_x, halo_y, edges, turn, cells, force, guests, push, tables, speeds, vertex,
    leave, bricks, meta, order, meta_sem, out_sem,
):
    faces = (x_near, x_far, y_near, y_far)
    odd_x, odd_y = parity("gx"), parity("gy")
    states = states_in.at[0, 0]
    copies = [
        pltpu.make_async_copy(faces[side].at[176:184, :], meta.at[side], meta_sem.at[side])
        for side in range(4)
    ] + [
        pltpu.make_async_copy(leave_hbm, leave, meta_sem.at[4]),
        pltpu.make_async_copy(bricks_hbm, bricks, meta_sem.at[5]),
    ]
    for copy in copies:
        copy.start()

    for side in range(4):
        for c in range(VERT // 128):
            for entry in range(9):
                guests[entry, 2 * side : 2 * side + 2, 128 * c : 128 * c + 128] = faces[side][
                    18 * c + 2 * entry : 18 * c + 2 * entry + 2, :
                ]

    for face, side in ((x_near, 1 - odd_x), (x_far, odd_x)):
        for i in range(5):
            at = FACE_ROWS + NZ * i
            halo_x[side, i] = face[at : at + NZ, :]
    row16 = rows((CX, CY))
    lane16 = lanes((CX, CY))
    near, far = [face[FACE_ROWS : FACE_ROWS + CX, :] for face in (y_near, y_far)]
    edges[1 - odd_y] = near
    edges[odd_y] = far
    for side, group in enumerate((Y_UP, Y_DOWN)):
        column = jnp.where(odd_y == 1, *((near, far) if side == 0 else (far, near)))
        for i, q in enumerate(group):
            cx = LATTICE[q][0]
            halo_y[side * 5 + i] = column if cx == 0 else pltpu.roll(column, cx % CX, 0)

    def pull(z, carry):
        density = None
        momentum = [None, None, None]
        at = pl.ds(pl.multiple_of(z * CX, CX), CX)
        for q in range(19):
            cx, cy, cz = LATTICE[q]
            source = (z - cz) & (NZ - 1)
            value = pops[q, pl.ds(pl.multiple_of(source * CX, CX), CX), :]
            if cx != 0:
                x = 0 if cx > 0 else CX - 1
                side, group = (0, X_UP) if cx > 0 else (1, X_DOWN)
                edge = halo_x[side, group.index(q), pl.ds(source, 1), :]
                value = jnp.where(
                    row16 == x, jnp.broadcast_to(edge, (CX, CY)), pltpu.roll(value, cx % CX, 0)
                )
            if cy != 0:
                side, group, pair = (0, Y_UP, EDGES_UP) if cy > 0 else (1, Y_DOWN, EDGES_DOWN)
                i = group.index(q)
                y = 0 if cy > 0 else CY - 1
                column = pltpu.roll(
                    halo_y[side * 5 + i], (y + 2 * CY - i * NZ - source) & (CY - 1), 1
                )
                if cx != 0:
                    n = [e[0] for e in pair].index(q)
                    corner = edges[side, pl.ds(source, 1), :]
                    corner = pltpu.roll(jnp.broadcast_to(corner, (CX, CY)), (y - 80 - n) % CY, 1)
                    column = jnp.where(row16 == x, corner, column)
                value = jnp.where(lane16 == y, column, pltpu.roll(value, cy % CY, 1))
            read[q, at, :] = value
            density = value if density is None else density + value
            for k, c in enumerate((cx, cy, cz)):
                if c != 0:
                    signed = value if c > 0 else -value
                    momentum[k] = signed if momentum[k] is None else momentum[k] + signed
        inverse = 1.0 / density
        flow[0, at, :] = density
        for k in range(3):
            flow[1 + k, at, :] = momentum[k]
            flow[4 + k, at, :] = momentum[k] * inverse
        return carry

    lax.fori_loop(0, NZ, pull, 0)

    left = lanes((16, 128)) < 64
    for k in range(3):
        for bz in range(2):
            tiles = [
                flow[4 + k, (8 * bz + iz) * CX + 8 * bx : (8 * bz + iz) * CX + 8 * bx + 8, :]
                for bx in range(2)
                for iz in range(8)
            ]
            turn[...] = jnp.concatenate(tiles, axis=0).T
            for j in range(4):
                even = turn[pl.ds(2 * j, 16, stride=8), :]
                odd = turn[pl.ds(2 * j + 1, 16, stride=8), :]
                pairs = (
                    jnp.where(left, even, pltpu.roll(odd, 64, 1)),
                    jnp.where(left, pltpu.roll(even, 64, 1), odd),
                )
                for bx in range(2):
                    base = (bz * 2 + bx) * 16 * 8
                    cells[j, pl.ds(base + k, 16, stride=8), :] = pairs[bx]

    stiff_product(push, guests, stiffness)
    force[...] = jnp.zeros(force.shape, F32)
    speeds[...] = jnp.zeros(speeds.shape, F32)
    for copy in copies:
        copy.wait()

    def sample_own(turn_number, carry):
        slot = order[turn_number]
        for chunk in range(VERT // CHUNK):
            at = slice(chunk * CHUNK, (chunk + 1) * CHUNK)
            table = tables.at[chunk % 2]
            fill_table(table, states, slot, at)
            homes = [
                pl.multiple_of(bricks[0, 0, slot, chunk * PER_CHUNK + b] * 8, 8)
                for b in range(PER_CHUNK)
            ]
            sample_chunk(speeds.at[0], cells, table, slot, at, homes)
        return carry

    def couple_guest(turn_number, carry):
        slot = order[turn_number]
        for chunk in range(VERT // CHUNK):
            at = slice(chunk * CHUNK, (chunk + 1) * CHUNK)
            table = tables.at[chunk % 2]
            fill_table(table, guests, slot, at)
            homes = [
                pl.multiple_of(
                    meta[slot // 2, 4 + slot % 2, chunk * PER_CHUNK + b].astype(jnp.int32) * 8, 8
                )
                for b in range(PER_CHUNK)
            ]
            sample_chunk(speeds.at[1], cells, table, slot, at, homes)
            spread_chunk(force, table, push, slot, at, homes)
        return carry

    stays = [leave[0, 0, slot] == 0 for slot in range(SLOTS)]
    lax.fori_loop(0, list_active(order, stays), sample_own, 0)
    arrives = [meta[slot // 2, 4 + slot % 2, 64] > 0.5 for slot in range(SLOTS)]
    lax.fori_loop(0, list_active(order, arrives), couple_guest, 0)

    row8 = rows((8, VERT))

    def by_side(value):
        pair = (row8 // 2) & 1
        turned = jnp.where(pair == 0, pltpu.roll(value, 6, 0), pltpu.roll(value, 2, 0))
        return jnp.where(jnp.where(row8 < 4, 1 - odd_x, 1 - odd_y) == 1, turned, value)

    for part, (source, flags) in enumerate(((states, stays), (guests, arrives))):
        active = jnp.zeros((8, VERT), jnp.int32)
        for slot, flag in enumerate(flags):
            active = jnp.where(row8 == slot, flag.astype(jnp.int32), active)
        span = slice(8 * part, 8 * part + 8)
        place = by_side if part == 1 else lambda value: value
        for k in range(3):
            speed = speeds[part, k]
            half = 0.5 * (source[6 + k] + speed)
            vertex[k, span, :] = place(jnp.where(active == 1, source[k] + half, 0.0))
            vertex[3 + k, span, :] = place(jnp.where(active == 1, source[3 + k] + half, 0.0))
            vertex[6 + k, span, :] = place(jnp.where(active == 1, speed, 0.0))
    vertex_copy = pltpu.make_async_copy(vertex, vertex_out.at[0, 0], out_sem.at[8])
    vertex_copy.start()

    for k in range(3):
        for bz in range(2):
            for j in range(4):
                base = bz * 2 * 16 * 8 + k
                zero = pl.ds(base, 16, stride=8)
                one = pl.ds(base + 128, 16, stride=8)
                zero = force[j, zero, :] + own_force[j, zero, :]
                one = force[j, one, :] + own_force[j, one, :]
                turn[pl.ds(2 * j, 16, stride=8), :] = jnp.where(left, zero, pltpu.roll(one, 64, 1))
                turn[pl.ds(2 * j + 1, 16, stride=8), :] = jnp.where(
                    left, pltpu.roll(zero, 64, 1), one
                )
            back = turn[...].T
            for bx in range(2):
                for iz in range(8):
                    first = (8 * bz + iz) * CX + 8 * bx
                    flow[4 + k, first : first + 8, :] = back[(bx * 8 + iz) * 8 : (bx * 8 + iz) * 8 + 8]

    def collide(z, carry):
        at = pl.ds(pl.multiple_of(z * CX, CX), CX)
        density = flow[0, at, :]
        inverse = 1.0 / density
        body = [flow[4 + k, at, :] for k in range(3)]
        speed = [(flow[1 + k, at, :] + 0.5 * body[k]) * inverse for k in range(3)]
        square = speed[0] * speed[0] + speed[1] * speed[1] + speed[2] * speed[2]
        work = speed[0] * body[0] + speed[1] * body[1] + speed[2] * body[2]
        common = density * (1.25 - 1.875 * square) - 1.125 * work
        wall = solid[at, :] == 1
        read[0, at, :] = jnp.where(wall, read[0, at, :], WEIGHTS[0] * common - 0.25 * read[0, at, :])
        steep = 5.625 * density
        slope = 3.75 * density
        for q in range(1, 19, 2):
            along, push_along = None, None
            for c, s, b in zip(LATTICE[q], speed, body):
                if c != 0:
                    s, b = (s, b) if c > 0 else (-s, -b)
                    along = s if along is None else along + s
                    push_along = b if push_along is None else push_along + b
            even = WEIGHTS[q] * (common + along * (steep * along + 3.375 * push_along))
            odd = WEIGHTS[q] * (slope * along + 1.125 * push_along)
            here, there = read[q, at, :], read[q + 1, at, :]
            read[q, at, :] = jnp.where(wall, there, even + odd - 0.25 * here)
            read[q + 1, at, :] = jnp.where(wall, here, even - odd - 0.25 * there)
        return carry

    def ship(part):
        span = slice(part * 32, (part + 1) * 32)
        return pltpu.make_async_copy(
            read.at[:, span, :], pops_out.at[:, span, :], out_sem.at[part]
        )

    for part in range(8):
        lax.fori_loop(part * 2, part * 2 + 2, collide, 0)
        ship(part).start()
    vertex_copy.wait()
    for part in range(8):
        ship(part).wait()


def step(leave, bricks, pops, solid, states, own_force, faces, stiffness):
    return pl.pallas_call(
        step_kernel,
        out_shape=[
            jax.ShapeDtypeStruct((19, NZ * CX, CY), F32),
            jax.ShapeDtypeStruct((1, 1, 9, ALL, VERT), F32),
        ],
        in_specs=[HBM, HBM] + [VMEM] * 9,
        out_specs=[HBM, HBM],
        scratch_shapes=[
            pltpu.VMEM((19, NZ * CX, CY), F32),
            pltpu.VMEM((7, NZ * CX, CY), F32),
            pltpu.VMEM((2, 5, NZ, CY), F32),
            pltpu.VMEM((10, CX, CY), F32),
            pltpu.VMEM((2, NZ, CY), F32),
            pltpu.VMEM((128, 128), F32),
            pltpu.VMEM((4, 512, 128), F32),
            pltpu.VMEM((4, 512, 128), F32),
            pltpu.VMEM((9, SLOTS, VERT), F32),
            pltpu.VMEM((24, VERT), F32),
            pltpu.VMEM((2, 512, CHUNK), BF16),
            pltpu.VMEM((2, 3, SLOTS, VERT), F32),
            pltpu.VMEM((9, ALL, VERT), F32),
            pltpu.SMEM((1, 1, SLOTS), jnp.int32),
            pltpu.SMEM((1, 1, SLOTS, BLOCKS), jnp.int32),
            pltpu.SMEM((4, 8, 128), F32),
            pltpu.SMEM((SLOTS + 1,), jnp.int32),
            pltpu.SemaphoreType.DMA((6,)),
            pltpu.SemaphoreType.DMA((9,)),
        ],
        compiler_params=pltpu.CompilerParams(vmem_limit_bytes=24 << 20),
        cost_estimate=pl.CostEstimate(
            flops=2 * 10**9, bytes_accessed=10**7, transcendentals=0
        ),
        name="lattice_step",
    )(leave, bricks, pops, solid, states, own_force, *faces, stiffness)


def exchange(x, axis, far):
    size = lax.axis_size(axis)
    return lax.ppermute(
        x, axis, [(i, (i + (1 if i % 2 == far else -1)) % size) for i in range(size)]
    )


def local(populations, solid_mask, bead_states, bead_bricks, leave_dir, stiffness):
    pops = populations.reshape(19, NZ * CX, CY)
    solid = solid_mask.reshape(NZ * CX, CY)
    states = bead_states.transpose(0, 1, 3, 2, 4)
    x_near, x_far = pack_x(leave_dir, bead_bricks, states, populations)
    x_far = exchange(x_far, "gx", 1)
    x_near = exchange(x_near, "gx", 0)
    y_near, y_far = pack_y(leave_dir, bead_bricks, states, populations)
    y_near, y_far = add_edges(y_near, y_far, x_near, x_far)
    y_far = exchange(y_far, "gy", 1)
    y_near = exchange(y_near, "gy", 0)
    own_force = spread_own(leave_dir, bead_bricks, states, stiffness)
    pops_out, vertex_out = step(
        leave_dir, bead_bricks, pops, solid, states, own_force,
        (x_near, x_far, y_near, y_far), stiffness,
    )
    return (pops_out.reshape(populations.shape), vertex_out.transpose(0, 1, 3, 2, 4))


def solution(mesh):
    return jax.shard_map(
        local,
        mesh=mesh,
        in_specs=(
            P(None, None, "gx", "gy"),
            P(None, "gx", "gy"),
            P("gx", "gy", None, None, None),
            P("gx", "gy", None, None),
            P("gx", "gy", None),
            P(),
        ),
        out_specs=(P(None, None, "gx", "gy"), P("gx", "gy", None, None, None)),
        check_vma=False,
    )
```

```python
import functools

import jax
import jax.numpy as jnp
import numpy as np
from jax import lax
from jax.experimental import pallas as pl
from jax.experimental.pallas import tpu as pltpu
from jax.sharding import PartitionSpec as P

LATTICE = [
    (0, 0, 0),
    (1, 0, 0),
    (-1, 0, 0),
    (0, 1, 0),
    (0, -1, 0),
    (0, 0, 1),
    (0, 0, -1),
    (1, 1, 0),
    (-1, -1, 0),
    (1, -1, 0),
    (-1, 1, 0),
    (1, 0, 1),
    (-1, 0, -1),
    (1, 0, -1),
    (-1, 0, 1),
    (0, 1, 1),
    (0, -1, -1),
    (0, 1, -1),
    (0, -1, 1),
]
WEIGHTS = [1.0 / 3.0] + [1.0 / 18.0] * 6 + [1.0 / 36.0] * 12
X_UP = [1, 7, 9, 11, 13]
X_DOWN = [2, 8, 10, 12, 14]
Y_UP = [3, 7, 10, 15, 17]
Y_DOWN = [4, 8, 9, 16, 18]
NZ, CX, CY = 16, 16, 128
SLOTS, SIDES, MIG, ALL = 8, 4, 2, 16
VERT, BLOCKS, CHUNK = 1280, 20, 256
F32, BF16 = jnp.float32, jnp.bfloat16


def lanes(shape):
    return lax.broadcasted_iota(jnp.int32, shape, len(shape) - 1)


def rows(shape):
    return lax.broadcasted_iota(jnp.int32, shape, len(shape) - 2)


BEAD_ROWS, FLAG_ROWS, FACE_ROWS = 180, 180, 184
X_ROWS, Y_ROWS = FACE_ROWS + 5 * NZ, FACE_ROWS + CX


def parity(axis):
    return lax.axis_index(axis) & 1


def pick(leave, code):
    first, second, count = jnp.int32(0), jnp.int32(0), jnp.int32(0)
    for slot in range(SLOTS):
        hit = leave[0, 0, slot] == code
        first = jnp.where(hit & (count == 0), slot, first)
        second = jnp.where(hit & (count == 1), slot, second)
        count = count + hit.astype(jnp.int32)
    return (first, second), count


def pack_beads(out, code, leave, bricks, states):
    chosen, count = pick(leave, code)
    out[176:184, :] = jnp.zeros((8, 128), F32)
    for place, slot in enumerate(chosen):
        for entry in range(9):
            row = states[entry, pl.ds(slot, 1), :]
            for c in range(VERT // 128):
                at = 18 * c + 2 * entry + place
                out[at : at + 1, :] = row[:, 128 * c : 128 * c + 128]
        valid = (count > place).astype(F32)
        at = FLAG_ROWS + place
        out[at : at + 1, :] = jnp.full((1, 128), 1.0, F32) * valid
        out[at : at + 1, 0:BLOCKS] = bricks[pl.ds(slot, 1), :].astype(F32)


def fetch_beads(leave_hbm, bricks_hbm, states_hbm, leave, bricks, states, sem):
    return [
        pltpu.make_async_copy(leave_hbm, leave, sem.at[0]),
        pltpu.make_async_copy(bricks_hbm.at[0, 0], bricks, sem.at[1]),
        pltpu.make_async_copy(states_hbm.at[0, 0], states, sem.at[2]),
    ]


def pack_x_kernel(
    leave_hbm, bricks_hbm, states_hbm, pops_hbm, near, far, leave, bricks, states, sem, face_sem
):
    copies = fetch_beads(leave_hbm, bricks_hbm, states_hbm, leave, bricks, states, sem)
    near_down = parity("gx")
    for n, (out, down) in enumerate(((near, near_down), (far, 1 - near_down))):
        x = (1 - down) * (CX - 1)
        for i, q in enumerate(X_UP):
            at = FACE_ROWS + NZ * i
            copies.append(
                pltpu.make_async_copy(
                    pops_hbm.at[q + down, :, x, :], out.at[at : at + NZ, :], face_sem.at[n * 5 + i]
                )
            )
    for copy in copies:
        copy.start()
    for copy in copies[:3]:
        copy.wait()
    pack_beads(near, 1 + near_down, leave, bricks, states)
    pack_beads(far, 2 - near_down, leave, bricks, states)
    for copy in copies[3:]:
        copy.wait()


Y_RANGES = ((3, 5), (7, 11), (15, 19))
Y_PLACE = {q: n for n, q in enumerate(q for lo, hi in Y_RANGES for q in range(lo, hi))}


def pack_y_kernel(
    leave_hbm, bricks_hbm, states_hbm, pops_hbm, near, far,
    leave, bricks, states, pops, sem, pops_sem,
):
    copies = fetch_beads(leave_hbm, bricks_hbm, states_hbm, leave, bricks, states, sem)
    for n, (lo, hi) in enumerate(Y_RANGES):
        at = Y_PLACE[lo]
        copies.append(
            pltpu.make_async_copy(
                pops_hbm.at[lo:hi], pops.at[at : at + hi - lo], pops_sem.at[n]
            )
        )
    for copy in copies:
        copy.start()
    for copy in copies[:3]:
        copy.wait()
    near_down = parity("gy")
    pack_beads(near, 3 + near_down, leave, bricks, states)
    pack_beads(far, 4 - near_down, leave, bricks, states)
    for copy in copies[3:]:
        copy.wait()
    lane = lanes((CX, CY))
    columns = []
    for group, y in ((Y_UP, CY - 1), (Y_DOWN, 0)):
        column = jnp.zeros((CX, CY), F32)
        for i, q in enumerate(group):
            for z in range(NZ):
                place = i * NZ + z
                column = jnp.where(
                    lane == place, pltpu.roll(pops[Y_PLACE[q], z], (place - y) % CY, 1), column
                )
        columns.append(column)
    near[FACE_ROWS : FACE_ROWS + CX, :] = jnp.where(near_down == 1, columns[1], columns[0])
    far[FACE_ROWS : FACE_ROWS + CX, :] = jnp.where(near_down == 1, columns[0], columns[1])


EDGES_UP = ((7, 0), (10, 1))
EDGES_DOWN = ((9, 0), (8, 1))


def edge_kernel(y_near, y_far, x_near, x_far, near_out, far_out):
    lane = lanes((NZ, CY))
    low_is_near = parity("gx") == 1
    near_down = parity("gy") == 1
    extra = []
    for edges, y in ((EDGES_UP, CY - 1), (EDGES_DOWN, 0)):
        column = jnp.zeros((NZ, CY), F32)
        for n, (q, side) in enumerate(edges):
            at = FACE_ROWS + NZ * (X_UP, X_DOWN)[side].index(q)
            near, far = x_near[at : at + NZ, :], x_far[at : at + NZ, :]
            face = jnp.where(low_is_near, *((near, far) if side == 0 else (far, near)))
            column = jnp.where(lane == 80 + n, pltpu.roll(face, (80 + n - y) % CY, 1), column)
        extra.append(column)
    up, down = extra
    for source, out, add in (
        (y_near, near_out, jnp.where(near_down, down, up)),
        (y_far, far_out, jnp.where(near_down, up, down)),
    ):
        out[0:FACE_ROWS, :] = source[0:FACE_ROWS, :]
        column = source[FACE_ROWS : FACE_ROWS + CX, :]
        out[FACE_ROWS : FACE_ROWS + CX, :] = jnp.where(lane < 80, column, add)


VMEM = pl.BlockSpec(memory_space=pltpu.VMEM)
HBM = pl.BlockSpec(memory_space=pltpu.HBM)
BEAD_SCRATCH = [
    pltpu.SMEM((1, 1, SLOTS), jnp.int32),
    pltpu.VMEM((SLOTS, BLOCKS), jnp.int32),
    pltpu.VMEM((9, SLOTS, VERT), F32),
]


def pack_x(leave, bricks, states, pops):
    return pl.pallas_call(
        pack_x_kernel,
        out_shape=[jax.ShapeDtypeStruct((X_ROWS, 128), F32)] * 2,
        in_specs=[HBM] * 4,
        out_specs=[VMEM] * 2,
        scratch_shapes=BEAD_SCRATCH
        + [pltpu.SemaphoreType.DMA((3,)), pltpu.SemaphoreType.DMA((10,))],
        compiler_params=pltpu.CompilerParams(vmem_limit_bytes=62 << 20),
        cost_estimate=pl.CostEstimate(flops=10**6, bytes_accessed=10**6, transcendentals=0),
        name="pack_x",
    )(leave, bricks, states, pops)


def pack_y(leave, bricks, states, pops):
    return pl.pallas_call(
        pack_y_kernel,
        out_shape=[jax.ShapeDtypeStruct((Y_ROWS, 128), F32)] * 2,
        in_specs=[HBM] * 4,
        out_specs=[VMEM] * 2,
        scratch_shapes=BEAD_SCRATCH
        + [
            pltpu.VMEM((10, NZ, CX, CY), F32),
            pltpu.SemaphoreType.DMA((3,)),
            pltpu.SemaphoreType.DMA((3,)),
        ],
        compiler_params=pltpu.CompilerParams(vmem_limit_bytes=8 << 20),
        cost_estimate=pl.CostEstimate(flops=10**6, bytes_accessed=2 * 10**6, transcendentals=0),
        name="pack_y",
    )(leave, bricks, states, pops)


def add_edges(y_near, y_far, x_near, x_far):
    return pl.pallas_call(
        edge_kernel,
        out_shape=[jax.ShapeDtypeStruct((Y_ROWS, 128), F32)] * 2,
        in_specs=[VMEM] * 4,
        out_specs=[VMEM] * 2,
        compiler_params=pltpu.CompilerParams(vmem_limit_bytes=8 << 20),
        name="add_edges",
    )(y_near, y_far, x_near, x_far)


def phi(distance):
    t = distance * distance
    value = jnp.full(t.shape, COSINE[-1], F32)
    for coefficient in COSINE[-2::-1]:
        value = value * t + coefficient
    return jnp.where(jnp.abs(distance) < 2.0, 0.5 * (value * value), 0.0)


def cosine_terms():
    terms, term = [], 1.0
    for n in range(8):
        terms.append(float(term))
        term = -term * (np.pi / 4) ** 2 / ((2 * n + 1) * (2 * n + 2))
    return terms


COSINE = cosine_terms()
PER_CHUNK = CHUNK // 64


def fill_table(table, states, slot, at):
    step8 = rows((8, CHUNK)).astype(F32)
    along_x, along_y, along_z = [
        phi(jnp.broadcast_to(states[k, pl.ds(slot, 1), at], (8, CHUNK)) - step8) for k in range(3)
    ]
    planes = [jnp.broadcast_to(along_z[iz : iz + 1, :], (8, CHUNK)) * along_x for iz in range(8)]
    for iy in range(8):
        factor = jnp.broadcast_to(along_y[iy : iy + 1, :], (8, CHUNK))
        for pair in range(4):
            both = jnp.concatenate(
                [planes[2 * pair] * factor, planes[2 * pair + 1] * factor], axis=0
            )
            first = iy * 64 + pair * 16
            table[first : first + 16, :] = both.astype(BF16)


def stiff_product(push, states, stiffness):
    shape = states[3:6].reshape(24, VERT).astype(BF16)
    for n in range(5):
        at = slice(n * 256, (n + 1) * 256)
        push[:, at] = -jnp.dot(shape, stiffness[:, at], preferred_element_type=F32)


def spread_product(table, push, slot, at):
    row8 = rows((8, CHUNK))
    block = lanes((8, CHUNK)) // 64
    parts = [
        jnp.broadcast_to(push[pl.ds(8 * k + slot, 1), at], (8, CHUNK)) for k in range(3)
    ]
    drive = jnp.where(row8 == 0, parts[0], jnp.where(row8 == 1, parts[1], parts[2]))
    drives = jnp.concatenate(
        [jnp.where(block == b, drive, 0.0) for b in range(PER_CHUNK)], axis=0
    ).astype(BF16)
    return lax.dot_general(
        drives, table[...], (((1,), (1,)), ((), ())), preferred_element_type=F32
    )


def spread_finish(force, spread, homes):
    for b, home in enumerate(homes):
        for j in range(4):
            force[j, pl.ds(home, 8), :] += spread[8 * b : 8 * b + 8, 128 * j : 128 * j + 128]


def sample_product(cells, table, homes):
    nearby = jnp.concatenate(
        [
            jnp.concatenate([cells[j, pl.ds(home, 8), :] for j in range(4)], axis=1)
            for home in homes
        ],
        axis=0,
    ).astype(BF16)
    return jnp.dot(nearby, table[...], preferred_element_type=F32)


def sample_finish(sampled_speed, sampled, slot, at):
    block = lanes((8, CHUNK)) // 64
    speed = sampled[0:8]
    for b in range(1, PER_CHUNK):
        speed = jnp.where(block == b, sampled[8 * b : 8 * b + 8], speed)
    for k in range(3):
        sampled_speed[k, pl.ds(slot, 1), at] = speed[k : k + 1, :]


CHUNKS = [slice(n * CHUNK, (n + 1) * CHUNK) for n in range(VERT // CHUNK)]


def list_active(order, flags):
    count = jnp.int32(0)
    for slot, flag in enumerate(flags):
        order[count] = slot
        count = count + flag.astype(jnp.int32)
    return count


def own_kernel(
    leave_hbm, bricks_hbm, states, stiffness, force, leave, bricks, push, tables, order, sem
):
    copies = [
        pltpu.make_async_copy(leave_hbm, leave, sem.at[0]),
        pltpu.make_async_copy(bricks_hbm, bricks, sem.at[1]),
    ]
    for copy in copies:
        copy.start()
    stiff_product(push, states.at[0, 0], stiffness)
    force[...] = jnp.zeros(force.shape, F32)
    for copy in copies:
        copy.wait()
    count = list_active(order, [leave[0, 0, slot] == 0 for slot in range(SLOTS)])

    def couple(turn_number, carry):
        slot = order[turn_number]
        for n, at in enumerate(CHUNKS):
            fill_table(tables.at[n], states.at[0, 0], slot, at)
        spreads = [spread_product(tables.at[n], push, slot, at) for n, at in enumerate(CHUNKS)]
        for n, spread in enumerate(spreads):
            homes = [
                pl.multiple_of(bricks[0, 0, slot, n * PER_CHUNK + b] * 8, 8)
                for b in range(PER_CHUNK)
            ]
            spread_finish(force, spread, homes)
        return carry

    lax.fori_loop(0, count, couple, 0)


def spread_own(leave, bricks, states, stiffness):
    return pl.pallas_call(
        own_kernel,
        out_shape=jax.ShapeDtypeStruct((4, 512, 128), F32),
        in_specs=[HBM, HBM, VMEM, VMEM],
        out_specs=VMEM,
        scratch_shapes=[
            pltpu.SMEM((1, 1, SLOTS), jnp.int32),
            pltpu.SMEM((1, 1, SLOTS, BLOCKS), jnp.int32),
            pltpu.VMEM((24, VERT), F32),
            pltpu.VMEM((VERT // CHUNK, 512, CHUNK), BF16),
            pltpu.SMEM((SLOTS + 1,), jnp.int32),
            pltpu.SemaphoreType.DMA((2,)),
        ],
        compiler_params=pltpu.CompilerParams(vmem_limit_bytes=16 << 20),
        cost_estimate=pl.CostEstimate(
            flops=2 * 10**9, bytes_accessed=5 * 10**6, transcendentals=0
        ),
        name="spread_own",
    )(leave, bricks, states, stiffness)


def step_kernel(
    leave_hbm, bricks_hbm, pops, solid, states_in, own_force,
    x_near, x_far, y_near, y_far,
    stiffness,
    pops_out, vertex_out,
    read, flow, halo_x, halo_y, edges, turn, cells, force, guests, push, tables, speeds, vertex,
    leave, bricks, meta, order, meta_sem, out_sem,
):
    faces = (x_near, x_far, y_near, y_far)
    odd_x, odd_y = parity("gx"), parity("gy")
    states = states_in.at[0, 0]
    copies = [
        pltpu.make_async_copy(faces[side].at[176:184, :], meta.at[side], meta_sem.at[side])
        for side in range(4)
    ] + [
        pltpu.make_async_copy(leave_hbm, leave, meta_sem.at[4]),
        pltpu.make_async_copy(bricks_hbm, bricks, meta_sem.at[5]),
    ]
    for copy in copies:
        copy.start()

    for side in range(4):
        for c in range(VERT // 128):
            for entry in range(9):
                guests[entry, 2 * side : 2 * side + 2, 128 * c : 128 * c + 128] = faces[side][
                    18 * c + 2 * entry : 18 * c + 2 * entry + 2, :
                ]

    for face, side in ((x_near, 1 - odd_x), (x_far, odd_x)):
        for i in range(5):
            at = FACE_ROWS + NZ * i
            halo_x[side, i] = face[at : at + NZ, :]
    row16 = rows((CX, CY))
    lane16 = lanes((CX, CY))
    near, far = [face[FACE_ROWS : FACE_ROWS + CX, :] for face in (y_near, y_far)]
    edges[1 - odd_y] = near
    edges[odd_y] = far
    for side, group in enumerate((Y_UP, Y_DOWN)):
        column = jnp.where(odd_y == 1, *((near, far) if side == 0 else (far, near)))
        for i, q in enumerate(group):
            cx = LATTICE[q][0]
            halo_y[side * 5 + i] = column if cx == 0 else pltpu.roll(column, cx % CX, 0)

    def pull(z, carry):
        density = None
        momentum = [None, None, None]
        at = pl.ds(pl.multiple_of(z * CX, CX), CX)
        for q in range(19):
            cx, cy, cz = LATTICE[q]
            source = (z - cz) & (NZ - 1)
            value = pops[q, pl.ds(pl.multiple_of(source * CX, CX), CX), :]
            if cx != 0:
                x = 0 if cx > 0 else CX - 1
                side, group = (0, X_UP) if cx > 0 else (1, X_DOWN)
                edge = halo_x[side, group.index(q), pl.ds(source, 1), :]
                value = jnp.where(
                    row16 == x, jnp.broadcast_to(edge, (CX, CY)), pltpu.roll(value, cx % CX, 0)
                )
            if cy != 0:
                side, group, pair = (0, Y_UP, EDGES_UP) if cy > 0 else (1, Y_DOWN, EDGES_DOWN)
                i = group.index(q)
                y = 0 if cy > 0 else CY - 1
                column = pltpu.roll(
                    halo_y[side * 5 + i], (y + 2 * CY - i * NZ - source) & (CY - 1), 1
                )
                if cx != 0:
                    n = [e[0] for e in pair].index(q)
                    corner = edges[side, pl.ds(source, 1), :]
                    corner = pltpu.roll(jnp.broadcast_to(corner, (CX, CY)), (y - 80 - n) % CY, 1)
                    column = jnp.where(row16 == x, corner, column)
                value = jnp.where(lane16 == y, column, pltpu.roll(value, cy % CY, 1))
            read[q, at, :] = value
            density = value if density is None else density + value
            for k, c in enumerate((cx, cy, cz)):
                if c != 0:
                    signed = value if c > 0 else -value
                    momentum[k] = signed if momentum[k] is None else momentum[k] + signed
        inverse = 1.0 / density
        flow[0, at, :] = density
        for k in range(3):
            flow[1 + k, at, :] = momentum[k]
            flow[4 + k, at, :] = momentum[k] * inverse
        return carry

    lax.fori_loop(0, NZ, pull, 0, unroll=True)

    left = lanes((16, 128)) < 64
    for k in range(3):
        for bz in range(2):
            tiles = [
                flow[4 + k, (8 * bz + iz) * CX + 8 * bx : (8 * bz + iz) * CX + 8 * bx + 8, :]
                for bx in range(2)
                for iz in range(8)
            ]
            turn[...] = jnp.concatenate(tiles, axis=0).T
            for j in range(4):
                even = turn[pl.ds(2 * j, 16, stride=8), :]
                odd = turn[pl.ds(2 * j + 1, 16, stride=8), :]
                pairs = (
                    jnp.where(left, even, pltpu.roll(odd, 64, 1)),
                    jnp.where(left, pltpu.roll(even, 64, 1), odd),
                )
                for bx in range(2):
                    base = (bz * 2 + bx) * 16 * 8
                    cells[j, pl.ds(base + k, 16, stride=8), :] = pairs[bx]

    stiff_product(push, guests, stiffness)
    force[...] = jnp.zeros(force.shape, F32)
    speeds[...] = jnp.zeros(speeds.shape, F32)
    for copy in copies:
        copy.wait()

    def sample_own(turn_number, carry):
        slot = order[turn_number]
        for n, at in enumerate(CHUNKS):
            fill_table(tables.at[n], states, slot, at)
        products = []
        for n in range(len(CHUNKS)):
            homes = [
                pl.multiple_of(bricks[0, 0, slot, n * PER_CHUNK + b] * 8, 8)
                for b in range(PER_CHUNK)
            ]
            products.append(sample_product(cells, tables.at[n], homes))
        for product, at in zip(products, CHUNKS):
            sample_finish(speeds.at[0], product, slot, at)
        return carry

    def couple_guest(turn_number, carry):
        slot = order[turn_number]
        for n, at in enumerate(CHUNKS):
            fill_table(tables.at[n], guests, slot, at)
        homes = [
            [
                pl.multiple_of(
                    meta[slot // 2, 4 + slot % 2, n * PER_CHUNK + b].astype(jnp.int32) * 8, 8
                )
                for b in range(PER_CHUNK)
            ]
            for n in range(len(CHUNKS))
        ]
        products = [
            (sample_product(cells, tables.at[n], homes[n]), spread_product(tables.at[n], push, slot, at))
            for n, at in enumerate(CHUNKS)
        ]
        for n, at in enumerate(CHUNKS):
            sample_finish(speeds.at[1], products[n][0], slot, at)
            spread_finish(force, products[n][1], homes[n])
        return carry

    stays = [leave[0, 0, slot] == 0 for slot in range(SLOTS)]
    lax.fori_loop(0, list_active(order, stays), sample_own, 0)
    arrives = [meta[slot // 2, 4 + slot % 2, 64] > 0.5 for slot in range(SLOTS)]
    lax.fori_loop(0, list_active(order, arrives), couple_guest, 0)

    row8 = rows((8, VERT))

    def by_side(value):
        pair = (row8 // 2) & 1
        turned = jnp.where(pair == 0, pltpu.roll(value, 6, 0), pltpu.roll(value, 2, 0))
        return jnp.where(jnp.where(row8 < 4, 1 - odd_x, 1 - odd_y) == 1, turned, value)

    for part, (source, flags) in enumerate(((states, stays), (guests, arrives))):
        active = jnp.zeros((8, VERT), jnp.int32)
        for slot, flag in enumerate(flags):
            active = jnp.where(row8 == slot, flag.astype(jnp.int32), active)
        span = slice(8 * part, 8 * part + 8)
        place = by_side if part == 1 else lambda value: value
        for k in range(3):
            speed = speeds[part, k]
            half = 0.5 * (source[6 + k] + speed)
            vertex[k, span, :] = place(jnp.where(active == 1, source[k] + half, 0.0))
            vertex[3 + k, span, :] = place(jnp.where(active == 1, source[3 + k] + half, 0.0))
            vertex[6 + k, span, :] = place(jnp.where(active == 1, speed, 0.0))
    vertex_copy = pltpu.make_async_copy(vertex, vertex_out.at[0, 0], out_sem.at[8])
    vertex_copy.start()

    for k in range(3):
        for bz in range(2):
            for j in range(4):
                base = bz * 2 * 16 * 8 + k
                zero = pl.ds(base, 16, stride=8)
                one = pl.ds(base + 128, 16, stride=8)
                zero = force[j, zero, :] + own_force[j, zero, :]
                one = force[j, one, :] + own_force[j, one, :]
                turn[pl.ds(2 * j, 16, stride=8), :] = jnp.where(left, zero, pltpu.roll(one, 64, 1))
                turn[pl.ds(2 * j + 1, 16, stride=8), :] = jnp.where(
                    left, pltpu.roll(zero, 64, 1), one
                )
            back = turn[...].T
            for bx in range(2):
                for iz in range(8):
                    first = (8 * bz + iz) * CX + 8 * bx
                    flow[4 + k, first : first + 8, :] = back[(bx * 8 + iz) * 8 : (bx * 8 + iz) * 8 + 8]

    def collide(z, carry):
        at = pl.ds(pl.multiple_of(z * CX, CX), CX)
        density = flow[0, at, :]
        inverse = 1.0 / density
        body = [flow[4 + k, at, :] for k in range(3)]
        speed = [(flow[1 + k, at, :] + 0.5 * body[k]) * inverse for k in range(3)]
        square = speed[0] * speed[0] + speed[1] * speed[1] + speed[2] * speed[2]
        work = speed[0] * body[0] + speed[1] * body[1] + speed[2] * body[2]
        common = density * (1.25 - 1.875 * square) - 1.125 * work
        wall = solid[at, :] == 1
        read[0, at, :] = jnp.where(wall, read[0, at, :], WEIGHTS[0] * common - 0.25 * read[0, at, :])
        steep = 5.625 * density
        slope = 3.75 * density
        for q in range(1, 19, 2):
            along, push_along = None, None
            for c, s, b in zip(LATTICE[q], speed, body):
                if c != 0:
                    s, b = (s, b) if c > 0 else (-s, -b)
                    along = s if along is None else along + s
                    push_along = b if push_along is None else push_along + b
            even = WEIGHTS[q] * (common + along * (steep * along + 3.375 * push_along))
            odd = WEIGHTS[q] * (slope * along + 1.125 * push_along)
            here, there = read[q, at, :], read[q + 1, at, :]
            read[q, at, :] = jnp.where(wall, there, even + odd - 0.25 * here)
            read[q + 1, at, :] = jnp.where(wall, here, even - odd - 0.25 * there)
        return carry

    def ship(part):
        span = slice(part * 32, (part + 1) * 32)
        return pltpu.make_async_copy(
            read.at[:, span, :], pops_out.at[:, span, :], out_sem.at[part]
        )

    for part in range(8):
        lax.fori_loop(part * 2, part * 2 + 2, collide, 0)
        ship(part).start()
    vertex_copy.wait()
    for part in range(8):
        ship(part).wait()


def step(leave, bricks, pops, solid, states, own_force, faces, stiffness):
    return pl.pallas_call(
        step_kernel,
        out_shape=[
            jax.ShapeDtypeStruct((19, NZ * CX, CY), F32),
            jax.ShapeDtypeStruct((1, 1, 9, ALL, VERT), F32),
        ],
        in_specs=[HBM, HBM] + [VMEM] * 9,
        out_specs=[HBM, HBM],
        scratch_shapes=[
            pltpu.VMEM((19, NZ * CX, CY), F32),
            pltpu.VMEM((7, NZ * CX, CY), F32),
            pltpu.VMEM((2, 5, NZ, CY), F32),
            pltpu.VMEM((10, CX, CY), F32),
            pltpu.VMEM((2, NZ, CY), F32),
            pltpu.VMEM((128, 128), F32),
            pltpu.VMEM((4, 512, 128), F32),
            pltpu.VMEM((4, 512, 128), F32),
            pltpu.VMEM((9, SLOTS, VERT), F32),
            pltpu.VMEM((24, VERT), F32),
            pltpu.VMEM((VERT // CHUNK, 512, CHUNK), BF16),
            pltpu.VMEM((2, 3, SLOTS, VERT), F32),
            pltpu.VMEM((9, ALL, VERT), F32),
            pltpu.SMEM((1, 1, SLOTS), jnp.int32),
            pltpu.SMEM((1, 1, SLOTS, BLOCKS), jnp.int32),
            pltpu.SMEM((4, 8, 128), F32),
            pltpu.SMEM((SLOTS + 1,), jnp.int32),
            pltpu.SemaphoreType.DMA((6,)),
            pltpu.SemaphoreType.DMA((9,)),
        ],
        compiler_params=pltpu.CompilerParams(vmem_limit_bytes=24 << 20),
        cost_estimate=pl.CostEstimate(
            flops=2 * 10**9, bytes_accessed=10**7, transcendentals=0
        ),
        name="lattice_step",
    )(leave, bricks, pops, solid, states, own_force, *faces, stiffness)


def exchange(x, axis, far):
    size = lax.axis_size(axis)
    return lax.ppermute(
        x, axis, [(i, (i + (1 if i % 2 == far else -1)) % size) for i in range(size)]
    )


def local(populations, solid_mask, bead_states, bead_bricks, leave_dir, stiffness):
    pops = populations.reshape(19, NZ * CX, CY)
    solid = solid_mask.reshape(NZ * CX, CY)
    states = bead_states.transpose(0, 1, 3, 2, 4)
    x_near, x_far = pack_x(leave_dir, bead_bricks, states, populations)
    x_far = exchange(x_far, "gx", 1)
    x_near = exchange(x_near, "gx", 0)
    y_near, y_far = pack_y(leave_dir, bead_bricks, states, populations)
    y_near, y_far = add_edges(y_near, y_far, x_near, x_far)
    y_far = exchange(y_far, "gy", 1)
    y_near = exchange(y_near, "gy", 0)
    own_force = spread_own(leave_dir, bead_bricks, states, stiffness)
    pops_out, vertex_out = step(
        leave_dir, bead_bricks, pops, solid, states, own_force,
        (x_near, x_far, y_near, y_far), stiffness,
    )
    return (pops_out.reshape(populations.shape), vertex_out.transpose(0, 1, 3, 2, 4))


def solution(mesh):
    return jax.shard_map(
        local,
        mesh=mesh,
        in_specs=(
            P(None, None, "gx", "gy"),
            P(None, "gx", "gy"),
            P("gx", "gy", None, None, None),
            P("gx", "gy", None, None),
            P("gx", "gy", None),
            P(),
        ),
        out_specs=(P(None, None, "gx", "gy"), P("gx", "gy", None, None, None)),
        check_vma=False,
    )
```

```python
import functools

import jax
import jax.numpy as jnp
import numpy as np
from jax import lax
from jax.experimental import pallas as pl
from jax.experimental.pallas import tpu as pltpu
from jax.sharding import PartitionSpec as P

LATTICE = [
    (0, 0, 0),
    (1, 0, 0),
    (-1, 0, 0),
    (0, 1, 0),
    (0, -1, 0),
    (0, 0, 1),
    (0, 0, -1),
    (1, 1, 0),
    (-1, -1, 0),
    (1, -1, 0),
    (-1, 1, 0),
    (1, 0, 1),
    (-1, 0, -1),
    (1, 0, -1),
    (-1, 0, 1),
    (0, 1, 1),
    (0, -1, -1),
    (0, 1, -1),
    (0, -1, 1),
]
WEIGHTS = [1.0 / 3.0] + [1.0 / 18.0] * 6 + [1.0 / 36.0] * 12
X_UP = [1, 7, 9, 11, 13]
X_DOWN = [2, 8, 10, 12, 14]
Y_UP = [3, 7, 10, 15, 17]
Y_DOWN = [4, 8, 9, 16, 18]
NZ, CX, CY = 16, 16, 128
SLOTS, SIDES, MIG, ALL = 8, 4, 2, 16
VERT, BLOCKS, CHUNK = 1280, 20, 256
F32, BF16 = jnp.float32, jnp.bfloat16


def lanes(shape):
    return lax.broadcasted_iota(jnp.int32, shape, len(shape) - 1)


def rows(shape):
    return lax.broadcasted_iota(jnp.int32, shape, len(shape) - 2)


BEAD_ROWS, FLAG_ROWS, FACE_ROWS = 180, 180, 184
X_ROWS, Y_ROWS = FACE_ROWS + 5 * NZ, FACE_ROWS + CX


def parity(axis):
    return lax.axis_index(axis) & 1


def pick(leave, code):
    first, second, count = jnp.int32(0), jnp.int32(0), jnp.int32(0)
    for slot in range(SLOTS):
        hit = leave[0, 0, slot] == code
        first = jnp.where(hit & (count == 0), slot, first)
        second = jnp.where(hit & (count == 1), slot, second)
        count = count + hit.astype(jnp.int32)
    return (first, second), count


def pack_beads(out, code, leave, bricks, states):
    chosen, count = pick(leave, code)
    out[176:184, :] = jnp.zeros((8, 128), F32)
    for place, slot in enumerate(chosen):
        for entry in range(9):
            row = states[entry, pl.ds(slot, 1), :]
            for c in range(VERT // 128):
                at = 18 * c + 2 * entry + place
                out[at : at + 1, :] = row[:, 128 * c : 128 * c + 128]
        valid = (count > place).astype(F32)
        at = FLAG_ROWS + place
        out[at : at + 1, :] = jnp.full((1, 128), 1.0, F32) * valid
        out[at : at + 1, 0:BLOCKS] = bricks[pl.ds(slot, 1), :].astype(F32)


def fetch_beads(leave_hbm, bricks_hbm, states_hbm, leave, bricks, states, sem):
    return [
        pltpu.make_async_copy(leave_hbm, leave, sem.at[0]),
        pltpu.make_async_copy(bricks_hbm.at[0, 0], bricks, sem.at[1]),
        pltpu.make_async_copy(states_hbm.at[0, 0], states, sem.at[2]),
    ]


def pack_x_kernel(
    leave_hbm, bricks_hbm, states_hbm, pops_hbm, near, far, leave, bricks, states, sem, face_sem
):
    copies = fetch_beads(leave_hbm, bricks_hbm, states_hbm, leave, bricks, states, sem)
    near_down = parity("gx")
    for n, (out, down) in enumerate(((near, near_down), (far, 1 - near_down))):
        x = (1 - down) * (CX - 1)
        for i, q in enumerate(X_UP):
            at = FACE_ROWS + NZ * i
            copies.append(
                pltpu.make_async_copy(
                    pops_hbm.at[q + down, :, x, :], out.at[at : at + NZ, :], face_sem.at[n * 5 + i]
                )
            )
    for copy in copies:
        copy.start()
    for copy in copies[:3]:
        copy.wait()
    pack_beads(near, 1 + near_down, leave, bricks, states)
    pack_beads(far, 2 - near_down, leave, bricks, states)
    for copy in copies[3:]:
        copy.wait()


Y_RANGES = ((3, 5), (7, 11), (15, 19))
Y_PLACE = {q: n for n, q in enumerate(q for lo, hi in Y_RANGES for q in range(lo, hi))}


def pack_y_kernel(
    leave_hbm, bricks_hbm, states_hbm, pops_hbm, near, far,
    leave, bricks, states, pops, sem, pops_sem,
):
    copies = fetch_beads(leave_hbm, bricks_hbm, states_hbm, leave, bricks, states, sem)
    for n, (lo, hi) in enumerate(Y_RANGES):
        at = Y_PLACE[lo]
        copies.append(
            pltpu.make_async_copy(
                pops_hbm.at[lo:hi], pops.at[at : at + hi - lo], pops_sem.at[n]
            )
        )
    for copy in copies:
        copy.start()
    for copy in copies[:3]:
        copy.wait()
    near_down = parity("gy")
    pack_beads(near, 3 + near_down, leave, bricks, states)
    pack_beads(far, 4 - near_down, leave, bricks, states)
    for copy in copies[3:]:
        copy.wait()
    lane = lanes((CX, CY))
    columns = []
    for group, y in ((Y_UP, CY - 1), (Y_DOWN, 0)):
        column = jnp.zeros((CX, CY), F32)
        for i, q in enumerate(group):
            for z in range(NZ):
                place = i * NZ + z
                column = jnp.where(
                    lane == place, pltpu.roll(pops[Y_PLACE[q], z], (place - y) % CY, 1), column
                )
        columns.append(column)
    near[FACE_ROWS : FACE_ROWS + CX, :] = jnp.where(near_down == 1, columns[1], columns[0])
    far[FACE_ROWS : FACE_ROWS + CX, :] = jnp.where(near_down == 1, columns[0], columns[1])


EDGES_UP = ((7, 0), (10, 1))
EDGES_DOWN = ((9, 0), (8, 1))


def edge_kernel(y_near, y_far, x_near, x_far, near_out, far_out):
    lane = lanes((NZ, CY))
    low_is_near = parity("gx") == 1
    near_down = parity("gy") == 1
    extra = []
    for edges, y in ((EDGES_UP, CY - 1), (EDGES_DOWN, 0)):
        column = jnp.zeros((NZ, CY), F32)
        for n, (q, side) in enumerate(edges):
            at = FACE_ROWS + NZ * (X_UP, X_DOWN)[side].index(q)
            near, far = x_near[at : at + NZ, :], x_far[at : at + NZ, :]
            face = jnp.where(low_is_near, *((near, far) if side == 0 else (far, near)))
            column = jnp.where(lane == 80 + n, pltpu.roll(face, (80 + n - y) % CY, 1), column)
        extra.append(column)
    up, down = extra
    for source, out, add in (
        (y_near, near_out, jnp.where(near_down, down, up)),
        (y_far, far_out, jnp.where(near_down, up, down)),
    ):
        out[0:FACE_ROWS, :] = source[0:FACE_ROWS, :]
        column = source[FACE_ROWS : FACE_ROWS + CX, :]
        out[FACE_ROWS : FACE_ROWS + CX, :] = jnp.where(lane < 80, column, add)


VMEM = pl.BlockSpec(memory_space=pltpu.VMEM)
HBM = pl.BlockSpec(memory_space=pltpu.HBM)
BEAD_SCRATCH = [
    pltpu.SMEM((1, 1, SLOTS), jnp.int32),
    pltpu.VMEM((SLOTS, BLOCKS), jnp.int32),
    pltpu.VMEM((9, SLOTS, VERT), F32),
]


def pack_x(leave, bricks, states, pops):
    return pl.pallas_call(
        pack_x_kernel,
        out_shape=[jax.ShapeDtypeStruct((X_ROWS, 128), F32)] * 2,
        in_specs=[HBM] * 4,
        out_specs=[VMEM] * 2,
        scratch_shapes=BEAD_SCRATCH
        + [pltpu.SemaphoreType.DMA((3,)), pltpu.SemaphoreType.DMA((10,))],
        compiler_params=pltpu.CompilerParams(vmem_limit_bytes=62 << 20),
        cost_estimate=pl.CostEstimate(flops=10**6, bytes_accessed=10**6, transcendentals=0),
        name="pack_x",
    )(leave, bricks, states, pops)


def pack_y(leave, bricks, states, pops):
    return pl.pallas_call(
        pack_y_kernel,
        out_shape=[jax.ShapeDtypeStruct((Y_ROWS, 128), F32)] * 2,
        in_specs=[HBM] * 4,
        out_specs=[VMEM] * 2,
        scratch_shapes=BEAD_SCRATCH
        + [
            pltpu.VMEM((10, NZ, CX, CY), F32),
            pltpu.SemaphoreType.DMA((3,)),
            pltpu.SemaphoreType.DMA((3,)),
        ],
        compiler_params=pltpu.CompilerParams(vmem_limit_bytes=8 << 20),
        cost_estimate=pl.CostEstimate(flops=10**6, bytes_accessed=2 * 10**6, transcendentals=0),
        name="pack_y",
    )(leave, bricks, states, pops)


def add_edges(y_near, y_far, x_near, x_far):
    return pl.pallas_call(
        edge_kernel,
        out_shape=[jax.ShapeDtypeStruct((Y_ROWS, 128), F32)] * 2,
        in_specs=[VMEM] * 4,
        out_specs=[VMEM] * 2,
        compiler_params=pltpu.CompilerParams(vmem_limit_bytes=8 << 20),
        name="add_edges",
    )(y_near, y_far, x_near, x_far)


def phi(distance):
    t = distance * distance
    value = jnp.full(t.shape, COSINE[-1], F32)
    for coefficient in COSINE[-2::-1]:
        value = value * t + coefficient
    return jnp.where(jnp.abs(distance) < 2.0, 0.5 * (value * value), 0.0)


def cosine_terms():
    terms, term = [], 1.0
    for n in range(8):
        terms.append(float(term))
        term = -term * (np.pi / 4) ** 2 / ((2 * n + 1) * (2 * n + 2))
    return terms


COSINE = cosine_terms()
PER_CHUNK = CHUNK // 64


def fill_table(table, states, slot, at):
    step8 = rows((8, CHUNK)).astype(F32)
    along_x, along_y, along_z = [
        phi(jnp.broadcast_to(states[k, pl.ds(slot, 1), at], (8, CHUNK)) - step8) for k in range(3)
    ]
    planes = [jnp.broadcast_to(along_z[iz : iz + 1, :], (8, CHUNK)) * along_x for iz in range(8)]
    for iy in range(8):
        factor = jnp.broadcast_to(along_y[iy : iy + 1, :], (8, CHUNK))
        for pair in range(4):
            both = jnp.concatenate(
                [planes[2 * pair] * factor, planes[2 * pair + 1] * factor], axis=0
            )
            first = iy * 64 + pair * 16
            table[first : first + 16, :] = both.astype(BF16)


def stiff_product(push, states, stiffness):
    shape = states[3:6].reshape(24, VERT).astype(BF16)
    for n in range(5):
        at = slice(n * 256, (n + 1) * 256)
        push[:, at] = -jnp.dot(shape, stiffness[:, at], preferred_element_type=F32)


def spread_product(table, push, slot, at):
    row8 = rows((8, CHUNK))
    block = lanes((8, CHUNK)) // 64
    parts = [
        jnp.broadcast_to(push[pl.ds(8 * k + slot, 1), at], (8, CHUNK)) for k in range(3)
    ]
    drive = jnp.where(row8 == 0, parts[0], jnp.where(row8 == 1, parts[1], parts[2]))
    drives = jnp.concatenate(
        [jnp.where(block == b, drive, 0.0) for b in range(PER_CHUNK)], axis=0
    ).astype(BF16)
    return lax.dot_general(
        drives, table[...], (((1,), (1,)), ((), ())), preferred_element_type=F32
    )


def spread_finish(force, spread, homes):
    for b, home in enumerate(homes):
        for j in range(4):
            force[j, pl.ds(home, 8), :] += spread[8 * b : 8 * b + 8, 128 * j : 128 * j + 128]


def sample_product(cells, table, homes):
    nearby = jnp.concatenate(
        [
            jnp.concatenate([cells[j, pl.ds(home, 8), :] for j in range(4)], axis=1)
            for home in homes
        ],
        axis=0,
    ).astype(BF16)
    return jnp.dot(nearby, table[...], preferred_element_type=F32)


def sample_finish(sampled_speed, sampled, slot, at):
    block = lanes((8, CHUNK)) // 64
    speed = sampled[0:8]
    for b in range(1, PER_CHUNK):
        speed = jnp.where(block == b, sampled[8 * b : 8 * b + 8], speed)
    for k in range(3):
        sampled_speed[k, pl.ds(slot, 1), at] = speed[k : k + 1, :]


CHUNKS = [slice(n * CHUNK, (n + 1) * CHUNK) for n in range(VERT // CHUNK)]


def list_active(order, flags):
    count = jnp.int32(0)
    for slot, flag in enumerate(flags):
        order[count] = slot
        count = count + flag.astype(jnp.int32)
    return count


def own_kernel(
    leave_hbm, bricks_hbm, states, stiffness, force, leave, bricks, push, tables, order, sem
):
    copies = [
        pltpu.make_async_copy(leave_hbm, leave, sem.at[0]),
        pltpu.make_async_copy(bricks_hbm, bricks, sem.at[1]),
    ]
    for copy in copies:
        copy.start()
    stiff_product(push, states.at[0, 0], stiffness)
    force[...] = jnp.zeros(force.shape, F32)
    for copy in copies:
        copy.wait()
    count = list_active(order, [leave[0, 0, slot] == 0 for slot in range(SLOTS)])

    def couple(turn_number, carry):
        slot = order[turn_number]
        for n, at in enumerate(CHUNKS):
            fill_table(tables.at[n], states.at[0, 0], slot, at)
        spreads = [spread_product(tables.at[n], push, slot, at) for n, at in enumerate(CHUNKS)]
        for n, spread in enumerate(spreads):
            homes = [
                pl.multiple_of(bricks[0, 0, slot, n * PER_CHUNK + b] * 8, 8)
                for b in range(PER_CHUNK)
            ]
            spread_finish(force, spread, homes)
        return carry

    lax.fori_loop(0, count, couple, 0)


def spread_own(leave, bricks, states, stiffness):
    return pl.pallas_call(
        own_kernel,
        out_shape=jax.ShapeDtypeStruct((4, 512, 128), F32),
        in_specs=[HBM, HBM, VMEM, VMEM],
        out_specs=VMEM,
        scratch_shapes=[
            pltpu.SMEM((1, 1, SLOTS), jnp.int32),
            pltpu.SMEM((1, 1, SLOTS, BLOCKS), jnp.int32),
            pltpu.VMEM((24, VERT), F32),
            pltpu.VMEM((VERT // CHUNK, 512, CHUNK), BF16),
            pltpu.SMEM((SLOTS + 1,), jnp.int32),
            pltpu.SemaphoreType.DMA((2,)),
        ],
        compiler_params=pltpu.CompilerParams(vmem_limit_bytes=16 << 20),
        cost_estimate=pl.CostEstimate(
            flops=2 * 10**9, bytes_accessed=5 * 10**6, transcendentals=0
        ),
        name="spread_own",
    )(leave, bricks, states, stiffness)


def step_kernel(
    leave_hbm, bricks_hbm, pops, solid, states_in, own_force,
    x_near, x_far, y_near, y_far,
    stiffness,
    pops_out, vertex_out,
    read, flow, halo_x, halo_y, edges, turn, cells, force, guests, push, tables, speeds, vertex,
    leave, bricks, meta, order, meta_sem, out_sem,
):
    faces = (x_near, x_far, y_near, y_far)
    odd_x, odd_y = parity("gx"), parity("gy")
    states = states_in.at[0, 0]
    copies = [
        pltpu.make_async_copy(faces[side].at[176:184, :], meta.at[side], meta_sem.at[side])
        for side in range(4)
    ] + [
        pltpu.make_async_copy(leave_hbm, leave, meta_sem.at[4]),
        pltpu.make_async_copy(bricks_hbm, bricks, meta_sem.at[5]),
    ]
    for copy in copies:
        copy.start()

    for side in range(4):
        for c in range(VERT // 128):
            for entry in range(9):
                guests[entry, 2 * side : 2 * side + 2, 128 * c : 128 * c + 128] = faces[side][
                    18 * c + 2 * entry : 18 * c + 2 * entry + 2, :
                ]

    for face, side in ((x_near, 1 - odd_x), (x_far, odd_x)):
        for i in range(5):
            at = FACE_ROWS + NZ * i
            halo_x[side, i] = face[at : at + NZ, :]
    row16 = rows((CX, CY))
    lane16 = lanes((CX, CY))
    near, far = [face[FACE_ROWS : FACE_ROWS + CX, :] for face in (y_near, y_far)]
    edges[1 - odd_y] = near
    edges[odd_y] = far
    for side, group in enumerate((Y_UP, Y_DOWN)):
        column = jnp.where(odd_y == 1, *((near, far) if side == 0 else (far, near)))
        for i, q in enumerate(group):
            cx = LATTICE[q][0]
            halo_y[side * 5 + i] = column if cx == 0 else pltpu.roll(column, cx % CX, 0)

    def pull(z, carry):
        density = None
        momentum = [None, None, None]
        at = pl.ds(pl.multiple_of(z * CX, CX), CX)
        for q in range(19):
            cx, cy, cz = LATTICE[q]
            source = (z - cz) & (NZ - 1)
            value = pops[q, pl.ds(pl.multiple_of(source * CX, CX), CX), :]
            if cx != 0:
                x = 0 if cx > 0 else CX - 1
                side, group = (0, X_UP) if cx > 0 else (1, X_DOWN)
                edge = halo_x[side, group.index(q), pl.ds(source, 1), :]
                value = jnp.where(
                    row16 == x, jnp.broadcast_to(edge, (CX, CY)), pltpu.roll(value, cx % CX, 0)
                )
            if cy != 0:
                side, group, pair = (0, Y_UP, EDGES_UP) if cy > 0 else (1, Y_DOWN, EDGES_DOWN)
                i = group.index(q)
                y = 0 if cy > 0 else CY - 1
                column = pltpu.roll(
                    halo_y[side * 5 + i], (y + 2 * CY - i * NZ - source) & (CY - 1), 1
                )
                if cx != 0:
                    n = [e[0] for e in pair].index(q)
                    corner = edges[side, pl.ds(source, 1), :]
                    corner = pltpu.roll(jnp.broadcast_to(corner, (CX, CY)), (y - 80 - n) % CY, 1)
                    column = jnp.where(row16 == x, corner, column)
                value = jnp.where(lane16 == y, column, pltpu.roll(value, cy % CY, 1))
            read[q, at, :] = value
            density = value if density is None else density + value
            for k, c in enumerate((cx, cy, cz)):
                if c != 0:
                    signed = value if c > 0 else -value
                    momentum[k] = signed if momentum[k] is None else momentum[k] + signed
        inverse = 1.0 / density
        flow[0, at, :] = density
        for k in range(3):
            flow[1 + k, at, :] = momentum[k]
            flow[4 + k, at, :] = momentum[k] * inverse
        return carry

    stiff_product(push, guests, stiffness)
    lax.fori_loop(0, NZ, pull, 0, unroll=True)

    left = lanes((16, 128)) < 64
    for k in range(3):
        for bz in range(2):
            tiles = [
                flow[4 + k, (8 * bz + iz) * CX + 8 * bx : (8 * bz + iz) * CX + 8 * bx + 8, :]
                for bx in range(2)
                for iz in range(8)
            ]
            turn[...] = jnp.concatenate(tiles, axis=0).T
            for j in range(4):
                even = turn[pl.ds(2 * j, 16, stride=8), :]
                odd = turn[pl.ds(2 * j + 1, 16, stride=8), :]
                pairs = (
                    jnp.where(left, even, pltpu.roll(odd, 64, 1)),
                    jnp.where(left, pltpu.roll(even, 64, 1), odd),
                )
                for bx in range(2):
                    base = (bz * 2 + bx) * 16 * 8
                    cells[j, pl.ds(base + k, 16, stride=8), :] = pairs[bx]

    force[...] = jnp.zeros(force.shape, F32)
    speeds[...] = jnp.zeros(speeds.shape, F32)
    for copy in copies:
        copy.wait()

    def sample_own(turn_number, carry):
        slot = order[turn_number]
        for n, at in enumerate(CHUNKS):
            fill_table(tables.at[n], states, slot, at)
        products = []
        for n in range(len(CHUNKS)):
            homes = [
                pl.multiple_of(bricks[0, 0, slot, n * PER_CHUNK + b] * 8, 8)
                for b in range(PER_CHUNK)
            ]
            products.append(sample_product(cells, tables.at[n], homes))
        for product, at in zip(products, CHUNKS):
            sample_finish(speeds.at[0], product, slot, at)
        return carry

    def couple_guest(turn_number, carry):
        slot = order[turn_number]
        for n, at in enumerate(CHUNKS):
            fill_table(tables.at[n], guests, slot, at)
        homes = [
            [
                pl.multiple_of(
                    meta[slot // 2, 4 + slot % 2, n * PER_CHUNK + b].astype(jnp.int32) * 8, 8
                )
                for b in range(PER_CHUNK)
            ]
            for n in range(len(CHUNKS))
        ]
        products = [
            (sample_product(cells, tables.at[n], homes[n]), spread_product(tables.at[n], push, slot, at))
            for n, at in enumerate(CHUNKS)
        ]
        for n, at in enumerate(CHUNKS):
            sample_finish(speeds.at[1], products[n][0], slot, at)
            spread_finish(force, products[n][1], homes[n])
        return carry

    stays = [leave[0, 0, slot] == 0 for slot in range(SLOTS)]
    lax.fori_loop(0, list_active(order, stays), sample_own, 0)
    arrives = [meta[slot // 2, 4 + slot % 2, 64] > 0.5 for slot in range(SLOTS)]
    lax.fori_loop(0, list_active(order, arrives), couple_guest, 0)

    row8 = rows((8, VERT))

    def by_side(value):
        pair = (row8 // 2) & 1
        turned = jnp.where(pair == 0, pltpu.roll(value, 6, 0), pltpu.roll(value, 2, 0))
        return jnp.where(jnp.where(row8 < 4, 1 - odd_x, 1 - odd_y) == 1, turned, value)

    for part, (source, flags) in enumerate(((states, stays), (guests, arrives))):
        active = jnp.zeros((8, VERT), jnp.int32)
        for slot, flag in enumerate(flags):
            active = jnp.where(row8 == slot, flag.astype(jnp.int32), active)
        span = slice(8 * part, 8 * part + 8)
        place = by_side if part == 1 else lambda value: value
        for k in range(3):
            speed = speeds[part, k]
            half = 0.5 * (source[6 + k] + speed)
            vertex[k, span, :] = place(jnp.where(active == 1, source[k] + half, 0.0))
            vertex[3 + k, span, :] = place(jnp.where(active == 1, source[3 + k] + half, 0.0))
            vertex[6 + k, span, :] = place(jnp.where(active == 1, speed, 0.0))
    vertex_copy = pltpu.make_async_copy(vertex, vertex_out.at[0, 0], out_sem.at[8])
    vertex_copy.start()

    for k in range(3):
        for bz in range(2):
            for j in range(4):
                base = bz * 2 * 16 * 8 + k
                zero = pl.ds(base, 16, stride=8)
                one = pl.ds(base + 128, 16, stride=8)
                zero = force[j, zero, :] + own_force[j, zero, :]
                one = force[j, one, :] + own_force[j, one, :]
                turn[pl.ds(2 * j, 16, stride=8), :] = jnp.where(left, zero, pltpu.roll(one, 64, 1))
                turn[pl.ds(2 * j + 1, 16, stride=8), :] = jnp.where(
                    left, pltpu.roll(zero, 64, 1), one
                )
            back = turn[...].T
            for bx in range(2):
                for iz in range(8):
                    first = (8 * bz + iz) * CX + 8 * bx
                    flow[4 + k, first : first + 8, :] = back[(bx * 8 + iz) * 8 : (bx * 8 + iz) * 8 + 8]

    def collide(z, carry):
        at = pl.ds(pl.multiple_of(z * CX, CX), CX)
        density = flow[0, at, :]
        inverse = 1.0 / density
        body = [flow[4 + k, at, :] for k in range(3)]
        speed = [(flow[1 + k, at, :] + 0.5 * body[k]) * inverse for k in range(3)]
        square = speed[0] * speed[0] + speed[1] * speed[1] + speed[2] * speed[2]
        work = speed[0] * body[0] + speed[1] * body[1] + speed[2] * body[2]
        common = density * (1.25 - 1.875 * square) - 1.125 * work
        wall = solid[at, :] == 1
        read[0, at, :] = jnp.where(wall, read[0, at, :], WEIGHTS[0] * common - 0.25 * read[0, at, :])
        steep = 5.625 * density
        slope = 3.75 * density
        for q in range(1, 19, 2):
            along, push_along = None, None
            for c, s, b in zip(LATTICE[q], speed, body):
                if c != 0:
                    s, b = (s, b) if c > 0 else (-s, -b)
                    along = s if along is None else along + s
                    push_along = b if push_along is None else push_along + b
            even = WEIGHTS[q] * (common + along * (steep * along + 3.375 * push_along))
            odd = WEIGHTS[q] * (slope * along + 1.125 * push_along)
            here, there = read[q, at, :], read[q + 1, at, :]
            read[q, at, :] = jnp.where(wall, there, even + odd - 0.25 * here)
            read[q + 1, at, :] = jnp.where(wall, here, even - odd - 0.25 * there)
        return carry

    def ship(part):
        span = slice(part * 32, (part + 1) * 32)
        return pltpu.make_async_copy(
            read.at[:, span, :], pops_out.at[:, span, :], out_sem.at[part]
        )

    for part in range(8):
        lax.fori_loop(part * 2, part * 2 + 2, collide, 0)
        ship(part).start()
    vertex_copy.wait()
    for part in range(8):
        ship(part).wait()


def step(leave, bricks, pops, solid, states, own_force, faces, stiffness):
    return pl.pallas_call(
        step_kernel,
        out_shape=[
            jax.ShapeDtypeStruct((19, NZ * CX, CY), F32),
            jax.ShapeDtypeStruct((1, 1, 9, ALL, VERT), F32),
        ],
        in_specs=[HBM, HBM] + [VMEM] * 9,
        out_specs=[HBM, HBM],
        scratch_shapes=[
            pltpu.VMEM((19, NZ * CX, CY), F32),
            pltpu.VMEM((7, NZ * CX, CY), F32),
            pltpu.VMEM((2, 5, NZ, CY), F32),
            pltpu.VMEM((10, CX, CY), F32),
            pltpu.VMEM((2, NZ, CY), F32),
            pltpu.VMEM((128, 128), F32),
            pltpu.VMEM((4, 512, 128), F32),
            pltpu.VMEM((4, 512, 128), F32),
            pltpu.VMEM((9, SLOTS, VERT), F32),
            pltpu.VMEM((24, VERT), F32),
            pltpu.VMEM((VERT // CHUNK, 512, CHUNK), BF16),
            pltpu.VMEM((2, 3, SLOTS, VERT), F32),
            pltpu.VMEM((9, ALL, VERT), F32),
            pltpu.SMEM((1, 1, SLOTS), jnp.int32),
            pltpu.SMEM((1, 1, SLOTS, BLOCKS), jnp.int32),
            pltpu.SMEM((4, 8, 128), F32),
            pltpu.SMEM((SLOTS + 1,), jnp.int32),
            pltpu.SemaphoreType.DMA((6,)),
            pltpu.SemaphoreType.DMA((9,)),
        ],
        compiler_params=pltpu.CompilerParams(vmem_limit_bytes=24 << 20),
        cost_estimate=pl.CostEstimate(
            flops=2 * 10**9, bytes_accessed=10**7, transcendentals=0
        ),
        name="lattice_step",
    )(leave, bricks, pops, solid, states, own_force, *faces, stiffness)


def exchange(x, axis, far):
    size = lax.axis_size(axis)
    return lax.ppermute(
        x, axis, [(i, (i + (1 if i % 2 == far else -1)) % size) for i in range(size)]
    )


def local(populations, solid_mask, bead_states, bead_bricks, leave_dir, stiffness):
    pops = populations.reshape(19, NZ * CX, CY)
    solid = solid_mask.reshape(NZ * CX, CY)
    states = bead_states.transpose(0, 1, 3, 2, 4)
    x_near, x_far = pack_x(leave_dir, bead_bricks, states, populations)
    x_far = exchange(x_far, "gx", 1)
    x_near = exchange(x_near, "gx", 0)
    y_near, y_far = pack_y(leave_dir, bead_bricks, states, populations)
    y_near, y_far = add_edges(y_near, y_far, x_near, x_far)
    y_far = exchange(y_far, "gy", 1)
    y_near = exchange(y_near, "gy", 0)
    own_force = spread_own(leave_dir, bead_bricks, states, stiffness)
    pops_out, vertex_out = step(
        leave_dir, bead_bricks, pops, solid, states, own_force,
        (x_near, x_far, y_near, y_far), stiffness,
    )
    return (pops_out.reshape(populations.shape), vertex_out.transpose(0, 1, 3, 2, 4))


def solution(mesh):
    return jax.shard_map(
        local,
        mesh=mesh,
        in_specs=(
            P(None, None, "gx", "gy"),
            P(None, "gx", "gy"),
            P("gx", "gy", None, None, None),
            P("gx", "gy", None, None),
            P("gx", "gy", None),
            P(),
        ),
        out_specs=(P(None, None, "gx", "gy"), P("gx", "gy", None, None, None)),
        check_vma=False,
    )
```
